128 devices in a mesh: cap: 16 (over y, x), tile: 8 (over z, core).
Axes of the slice: x: 4, y: 4, z: 4, core: 2. Of those that a mesh axis runs over, the one named last changes fastest.
Arguments:
- load: float32 [3, 32, 1536, 128], P(None, 'cap', 'tile'), may hold values from -6 to 6
- previous: float32 [3, 32, 1536, 128], P(None, 'cap', 'tile'), may hold values from -4 to 4
- stress_old: float32 [12, 32, 1536, 128], P(None, 'cap', 'tile'), may hold values from -6 to 6
- shear_modulus: float32 [32, 1536, 128], P('cap', 'tile'), may hold values from 0.5 to 5
- relaxation: float32 [32, 1536, 128], P('cap', 'tile'), may hold values from 0.05 to 2
- density_jump: float32 [32], P('cap'), may hold values from 0.2 to 2
- element_stiffness: float32 [12, 12], replicated, may hold values from -2.9 to 3.4, as said below
- degree_slots: int32 [768], replicated, may hold values from 0 to 767, each once
Outputs:
- displacement: float32 [3, 32, 1536, 128], P(None, 'cap', 'tile')
- stress_new: float32 [12, 32, 1536, 128], P(None, 'cap', 'tile')
- potential_coeffs: float32 [768, 32, 256], P('tile', 'cap')
The draws below stay inside these ranges and needn't reach their ends.
Inputs may be any that keep to these rules, and one draw needn't show every extreme that they name: `element_stiffness`: symmetric positive definite. `degree_slots`: each degree 0 to 767 sits in exactly one slot.
All inputs are finite; a program needn't handle non-finite values.
Results may differ from the reference program's by a relative error of at most 0.00013.
Values sent between devices are 32-bit elements; how exact they have to be, the bound alone decides.
No kernel may reach another device: no remote copies, remote signals or barrier semaphores. Data moves between devices by JAX's collectives and lax.ppermute only.
A program may use at most 128 MiB of HBM per device.

```python
import math
import jax
import jax.numpy as jnp
from jax import lax

S = 128
HRING = 1536
LDEG = 768
ITERS = 6
NR = 32


def draw_element_stiffness(key, part):
    factors = jax.random.uniform(key, (12, 12), jnp.float32, -1.7, 1.7)
    return jnp.dot(factors, factors.T) / 12.0 + 0.5 * jnp.eye(12, dtype=jnp.float32)


def steps_of(own_key, extent, pieces, smallest, top_value):
    gain, own = 1.0, jax.random.fold_in(own_key, 6)
    for dim, parts in pieces:
        steps = jnp.exp(jax.random.uniform(jax.random.fold_in(own, dim), (parts,), jnp.float32, smallest / len(pieces), top_value / len(pieces)))
        gain = gain * jnp.repeat(steps, extent[dim] // parts).reshape([-1 if axis == dim else 1 for axis in range(len(extent))])
    return gain


def bell_draw(own_key, dims, width, limit, shards=(), kind=jnp.bfloat16):
    gain = steps_of(own_key, dims, shards, -0.22, 0.18) if shards else 1.0
    drawn = jax.random.normal(own_key, dims, jnp.float32) * width * gain
    return jnp.minimum(jnp.maximum(drawn, -limit), limit).astype(kind)


def setup_inputs(seed: int = 0) -> dict:
    streams_of = jax.random.split(jax.random.key(seed), 9)
    load = bell_draw(streams_of[0], (3, NR, HRING, S), 1.0, 6.0, ((1, 16), (2, 8)), jnp.float32)
    previous = bell_draw(streams_of[1], (3, NR, HRING, S), 0.5, 4.0, ((1, 16), (2, 8)), jnp.float32)
    stress_old = bell_draw(streams_of[2], (12, NR, HRING, S), 1.0, 6.0, ((1, 16), (2, 8)), jnp.float32)
    shear_modulus = jnp.clip(jnp.exp(math.log(5.0) - 2.3025851 * jax.random.uniform(streams_of[3], (NR, HRING, S), jnp.float32) ** steps_of(streams_of[3], (NR, HRING, S), ((0, 16), (1, 8)), -0.2, 0.2)), 0.5, 5.0)
    relaxation = jnp.clip(jnp.exp(math.log(2.0) - 3.6888794 * jax.random.uniform(streams_of[4], (NR, HRING, S), jnp.float32) ** steps_of(streams_of[4], (NR, HRING, S), ((0, 16), (1, 8)), -0.2, 0.2)), 0.05, 2.0)
    density_jump = jnp.clip(jnp.exp(math.log(2.0) - 2.3025851 * jax.random.uniform(streams_of[5], (NR,), jnp.float32) ** steps_of(streams_of[5], (NR,), ((0, 16),), -0.2, 0.2)), 0.2, 2.0)
    element_stiffness = draw_element_stiffness(jax.random.fold_in(streams_of[8], 71), 0)
    degree_slots = jax.random.permutation(streams_of[7], LDEG).astype(jnp.int32)
    return dict(load=load, previous=previous, stress_old=stress_old, shear_modulus=shear_modulus, relaxation=relaxation, density_jump=density_jump, element_stiffness=element_stiffness, degree_slots=degree_slots)


precise = lax.Precision.HIGHEST
rotation_gain = 2.0
gravity_gain = 0.2

def radius_rows(offset, amount, layers):
    positions = (offset + jnp.arange(amount, dtype=jnp.int32)).astype(jnp.float32)
    return 1.0 - 0.45 * (positions + 0.5) / layers

def cycle_basis(degrees, columns):
    windings = degrees[:, None] * columns[None, :] % HRING
    angles = windings.astype(jnp.float32) * (2.0 * math.pi / HRING)
    return (jnp.cos(angles), jnp.sin(angles))

def green_kernel(degrees, target_radius, source_radius):
    degree_float = degrees.astype(jnp.float32)
    distance = jnp.abs(jnp.log(target_radius)[:, None] - jnp.log(source_radius)[None, :])
    return jnp.exp(-degree_float[:, None, None] * distance[None]) / jnp.sqrt(2.0 * degree_float + 1.0)[:, None, None]

def rotation_term(degrees, radius_list, moment):
    selector = (degrees == 2).astype(jnp.float32)
    return rotation_gain * selector[:, None, None] * (radius_list ** 2)[None, :, None] * moment[:, None, :]

def corner_values(nodal_field):
    padded = jnp.concatenate([nodal_field, jnp.zeros_like(nodal_field[:, :1])], axis=1)
    shallow = padded[:, :-1]
    deeper = padded[:, 1:]
    stacked = jnp.stack([shallow, jnp.roll(shallow, -1, axis=2), deeper, jnp.roll(deeper, -1, axis=2)], axis=1)
    return stacked.reshape((12,) + nodal_field.shape[1:])

def assemble(forces):
    grouped = forces.reshape((3, 4) + forces.shape[1:])
    shallow = grouped[:, 0] + jnp.roll(grouped[:, 1], 1, axis=2)
    deeper = grouped[:, 2] + jnp.roll(grouped[:, 3], 1, axis=2)
    moved = jnp.concatenate([jnp.zeros_like(deeper[:, :1]), deeper[:, :-1]], axis=1)
    return shallow + moved

def element_forces(nodal_field, stiffness, effective):
    return effective[None] * jnp.einsum('ab,brhs->arhs', stiffness, corner_values(nodal_field), precision=precise)

def reference(load, previous, stress_old, shear_modulus, relaxation, density_jump, element_stiffness, degree_slots):
    effective = shear_modulus / (1.0 + 0.5 * relaxation)
    carried_share = relaxation / (1.0 + 0.5 * relaxation)
    retained = (1.0 - 0.5 * relaxation) / (1.0 + 0.5 * relaxation)
    radius_all = radius_rows(0, NR, NR)
    columns = jnp.arange(HRING, dtype=jnp.int32)
    cosine, sine_table = cycle_basis(degree_slots, columns)
    weighted = previous[0] * density_jump[:, None, None]
    normalizer = math.sqrt(2.0 / HRING)
    first_half = jnp.einsum('kh,rhs->krs', cosine, weighted, precision=precise)
    second_half = jnp.einsum('kh,rhs->krs', sine_table, weighted, precision=precise)
    coefficients = jnp.concatenate([first_half, second_half], axis=2) * normalizer
    kernel = green_kernel(degree_slots, radius_all, radius_all)
    moment = jnp.einsum('j,kjs->ks', radius_all ** 4 / NR, coefficients, precision=precise)
    potential = jnp.einsum('kij,kjs->kis', kernel, coefficients, precision=precise)
    potential = potential + rotation_term(degree_slots, radius_all, moment)
    potential_field = jnp.einsum('krs,kh->rhs', potential[:, :, :S], cosine, precision=precise)
    potential_field = potential_field + jnp.einsum('krs,kh->rhs', potential[:, :, S:], sine_table, precision=precise)
    gravity_force = gravity_gain * density_jump[:, None, None] * potential_field
    right_side = load + assemble(carried_share[None] * stress_old)
    right_side = right_side + jnp.concatenate([gravity_force[None], jnp.zeros_like(load[1:])], axis=0)

    def operate(vector):
        return assemble(element_forces(vector, element_stiffness, effective))
    residual = right_side - operate(previous)
    norm_start = jnp.sum(residual * residual)

    def iterate(counter, carry_state):
        solution, residual, direction, norm_now = carry_state
        applied = operate(direction)
        step_size = norm_now / jnp.sum(direction * applied)
        solution = solution + step_size * direction
        residual = residual - step_size * applied
        norm_next = jnp.sum(residual * residual)
        direction = residual + norm_next / norm_now * direction
        return (solution, residual, direction, norm_next)
    solution = lax.fori_loop(0, ITERS, iterate, (previous, residual, residual, norm_start))[0]
    stress_new = retained[None] * stress_old + element_forces(solution, element_stiffness, effective)
    return (solution, stress_new, potential)
```

```python
import functools
import math

import jax
import jax.numpy as jnp
import ml_dtypes
import numpy as np
from jax import lax
from jax.experimental import pallas as pl
from jax.experimental.pallas import tpu as pltpu
from jax.sharding import Mesh
from jax.sharding import PartitionSpec as P

HRING = 1536
LDEG = 768
NR = 32
TILE = ("tile_0", "tile_1")
CAP = ("cap_0", "cap_1")
ALL = ("cap_0", "cap_1", "tile_0", "tile_1")
LANES = 128
COLS = 192
ROOT3H = math.sqrt(3.0) / 2.0
rotation_gain = 2.0
gravity_gain = 0.2

EFF_TILE = 21
TAIL_TILE = 24
IN_TILES = 26
OUT_TAIL = 12
OUT_TILES = 14

f32 = jnp.float32
bf16 = jnp.bfloat16


def split_table(table):
    high = table.astype(ml_dtypes.bfloat16)
    low = (table - high.astype(np.float64)).astype(ml_dtypes.bfloat16)
    return high, low


def transform_tables():
    q = np.arange(128)[None, :]
    b = np.arange(256)[:, None]
    angle = 2.0 * np.pi * ((q * b) % 256) / 256.0
    cosine, sine = np.cos(angle), np.sin(angle)
    table = np.concatenate(
        [np.concatenate([cosine, sine], 1), np.concatenate([sine, -cosine], 1)], 0
    )
    p = np.arange(8)[:, None]
    turn = 2.0 * np.pi * ((p * np.arange(256)[None, :]) % HRING) / HRING
    twiddle = np.stack([np.cos(turn), np.sin(turn)]).astype(np.float32)
    return split_table(table), split_table(np.ascontiguousarray(table.T)), twiddle


def radial_tables():
    radius = 1.0 - 0.45 * (np.arange(NR) + 0.5) / NR
    degree = 6.0 * np.arange(128)[None, :] + np.arange(8)[:, None]
    log_radius = np.log(radius)
    ratio = np.zeros((NR, 8, 128))
    for r in range(1, NR):
        ratio[r] = np.exp(-degree * (log_radius[r - 1] - log_radius[r]))
    scale = 1.0 / np.sqrt(2.0 * degree + 1.0)
    return ratio.astype(np.float32), scale.astype(np.float32), radius


def split(x):
    high = x.astype(bf16)
    return high, (x - high.astype(f32)).astype(bf16)


def mm(a, b):
    return jnp.dot(a, b, preferred_element_type=f32)


def lane_index(shape):
    return lax.broadcasted_iota(jnp.int32, shape, len(shape) - 1)


def row_index(shape):
    return lax.broadcasted_iota(jnp.int32, shape, 0)


def tile_of(k):
    return slice(k * LANES, (k + 1) * LANES)


def down_one(x):
    return jnp.where(row_index(x.shape) == 0, 0.0, pltpu.roll(x, 1, 0))


def up_one(x):
    n = x.shape[0]
    return jnp.where(row_index(x.shape) == n - 1, 0.0, pltpu.roll(x, n - 1, 0))


def pack_kernel(parity_ref, density_ref, load_ref, prev_ref, stress_ref, shear_ref, relax_ref,
                out_ref, acc_ref, tail_ref):
    comp = pl.program_id(0)
    parity = parity_ref[0]
    wide = pl.ds(pl.multiple_of(64 * parity, 64), 128)
    narrow = pl.ds(pl.multiple_of(128 * (1 - parity), 64), 64)

    def put(tile, block):
        start = pl.multiple_of(tile * LANES, LANES)
        out_ref[:, pl.ds(start, LANES)] = jnp.transpose(block)

    @pl.when(comp == 0)
    def _():
        acc_ref[:2] = shear_ref[...] / (1.0 + 0.5 * relax_ref[...])
        put(EFF_TILE, acc_ref[0, wide, :])
        put(EFF_TILE + 1, acc_ref[1, wide, :])
        put(EFF_TILE + 2, jnp.concatenate([acc_ref[0, narrow, :], acc_ref[1, narrow, :]], 0))
        tail_ref[192:256, :] = jnp.zeros((64, LANES), f32)
        for r in range(2):
            tail_ref[201 + r : 202 + r, :] = jnp.full((1, LANES), density_ref[r], f32)

    base = comp * 7
    put(base, prev_ref[0, 0, wide, :])
    put(base + 1, prev_ref[0, 1, wide, :])
    put(base + 2, jnp.concatenate([prev_ref[0, 0, narrow, :], prev_ref[0, 1, narrow, :]], 0))

    relax = relax_ref[...]
    carried = relax / (1.0 + 0.5 * relax)
    part = [[carried[r] * stress_ref[q, r] for r in range(2)] for q in range(4)]
    near = [part[0][0], part[0][1] + part[2][0], part[2][1]]
    far = [part[1][0], part[1][1] + part[3][0], part[3][1]]
    for r in range(3):
        total = near[r] + down_one(far[r])
        if r < 2:
            total = total + load_ref[0, r]
        acc_ref[r] = total
        tail_ref[pl.ds(192 + 3 * comp + r, 1), :] = far[r][COLS - 1 : COLS, :]
    for r in range(3):
        put(base + 3 + r, acc_ref[r, wide, :])
    put(base + 6, jnp.concatenate([acc_ref[0, narrow, :], acc_ref[1, narrow, :]], 0))
    tail_ref[pl.ds(pl.multiple_of(64 * comp, 64), 64), :] = acc_ref[2, narrow, :]

    @pl.when(comp == 2)
    def _():
        put(TAIL_TILE, tail_ref[:128, :])
        put(TAIL_TILE + 1, tail_ref[128:, :])


def section_kernel(stiff_ref, recv_ref, slots_ref, fh_ref, fl_ref, th_ref, tl_ref, twiddle_ref,
                   ratio_ref, scale_ref, basis_ref, send_ref,
                   eff_ref, matrix_ref, xh_ref, xl_ref, image_ref, coef_ref, pot_ref, stage_ref,
                   *, radius):
    lane = lane_index((16, LANES))
    for k in range(IN_TILES):
        stage_ref[tile_of(k), :] = recv_ref[:, tile_of(k)]

    def rows_of(t, tile):
        return stage_ref[pl.ds(LANES * tile + t, 16, stride=8), :]

    def unrolled(wide_tile, narrow_tile, half):
        for u in range(4):
            even, odd = rows_of(2 * u, narrow_tile), rows_of(2 * u + 1, narrow_tile)
            if half == 0:
                middle = jnp.where(lane < 64, even, pltpu.roll(odd, 64, 1))
            else:
                middle = jnp.where(lane < 64, pltpu.roll(even, 64, 1), odd)
            yield 3 * u, rows_of(2 * u, wide_tile)
            yield 3 * u + 1, middle
            yield 3 * u + 2, rows_of(2 * u + 1, wide_tile)

    tail = TAIL_TILE
    for c in range(3):
        for r in range(2):
            rows = slice(32 * c + 16 * r, 32 * c + 16 * r + 16)
            for k, block in unrolled(7 * c + r, 7 * c + 2, r):
                basis_ref[1, rows, tile_of(k)] = block
            for k, block in unrolled(7 * c + 3 + r, 7 * c + 6, r):
                basis_ref[0, rows, tile_of(k)] = block
        rows = slice(32 * c, 32 * c + 16)
        for k, block in unrolled(7 * c + 5, tail + c // 2, c % 2):
            basis_ref[0, rows, tile_of(k)] += down_one(block)
    for t in range(8):
        following = (t + 1) % 8
        k, target = 3 * (following // 2) + following % 2, 64 * (following % 2)
        block = rows_of(t, tail + 1)
        for c in range(3):
            for r in range(3):
                shift = (target - 64 - 3 * c - r) % LANES
                value = jnp.where(lane == target, pltpu.roll(block, shift, 1), 0.0)
                if r == 2:
                    value = down_one(value)
                start = 32 * c + 16 * (r % 2)
                basis_ref[0, start : start + 16, tile_of(k)] += value
    for r in range(2):
        for k, block in unrolled(EFF_TILE + r, EFF_TILE + 2, r):
            eff_ref[0, 16 * r : 16 * r + 16, tile_of(k)] = block
    eff_ref[1, 16:32, :] = eff_ref[0, 0:16, :]
    eff_ref[1, 0:16, :] = down_one(eff_ref[0, 16:32, :])
    eff_ref[2] = pltpu.roll(eff_ref[0], 1, 1)
    eff_ref[3] = pltpu.roll(eff_ref[1], 1, 1)

    density = jnp.concatenate(
        [jnp.sum(jnp.where(lane == 73 + r, rows_of(0, tail + 1), 0.0), 1, keepdims=True)
         for r in range(2)], 0
    )

    weight = density * math.sqrt(2.0 / HRING)
    w = [basis_ref[1, 0:32, 256 * a : 256 * a + 256] * weight for a in range(6)]
    s1, s2, d1, d2 = w[1] + w[5], w[2] + w[4], w[1] - w[5], w[2] - w[4]
    plus, minus = w[0] + w[3], w[0] - w[3]
    half = 0.5 * (s1 + s2)
    diff = 0.5 * (s1 - s2)
    real = [plus + 2.0 * half, minus + diff, plus - half, minus - 2.0 * diff]
    real += [real[2], real[1]]
    i1, i2 = -ROOT3H * (d1 + d2), -ROOT3H * (d1 - d2)
    imag = [None, i1, i2, None, -i2, -i1]
    for p in range(6):
        cosine, sine = twiddle_ref[0, p : p + 1, :], twiddle_ref[1, p : p + 1, :]
        rows = slice(32 * p, 32 * p + 32)
        re, im = real[p] * cosine, -real[p] * sine
        if imag[p] is not None:
            re, im = re + imag[p] * sine, im + imag[p] * cosine
        for k, x in ((0, re), (256, im)):
            high, low = split(x)
            xh_ref[rows, k : k + 256] = high
            xl_ref[rows, k : k + 256] = low
    high, low = xh_ref[0:192, 0:512], xl_ref[0:192, 0:512]
    coefs = mm(high, fh_ref[...]) + mm(low, fh_ref[...]) + mm(high, fl_ref[...])
    for k in range(2):
        coef_ref[256 * k : 256 * k + 192, :] = coefs[:, tile_of(k)]
        coef_ref[256 * k + 192 : 256 * k + 256, :] = jnp.zeros((64, LANES), f32)

    def place(r, k):
        return pl.ds(256 * k + 16 * (r % 2) + r // 2, 8, stride=32)

    zero = jnp.zeros((8, LANES), f32)
    for k in range(2):
        lanes = tile_of(k)
        rows = [coef_ref[place(r, k), :] for r in range(NR)]
        forward, moment = zero, zero
        for r in range(NR):
            forward = rows[r] + ratio_ref[r] * forward
            moment = moment + (radius[r] ** 4 / NR) * rows[r]
            pot_ref[r, :, lanes] = forward
        chosen = (lane_index((8, LANES)) == 0) & (row_index((8, LANES)) == 2)
        moment = jnp.where(chosen, rotation_gain * moment, 0.0)
        back = zero
        for r in reversed(range(NR)):
            if r + 1 < NR:
                back = ratio_ref[r + 1] * (rows[r + 1] + back)
            pot_ref[r, :, lanes] = (
                (pot_ref[r, :, lanes] + back) * scale_ref[...] + radius[r] ** 2 * moment
            )
    for k in range(2):
        for r in range(NR):
            coef_ref[place(r, k), :] = pot_ref[r, :, tile_of(k)]

    for k in range(2):
        for p in range(6):
            x = coef_ref[256 * k + 32 * p : 256 * k + 32 * p + 32, :]
            high, low = split(x)
            rest = (x - high.astype(f32) - low.astype(f32)).astype(bf16)
            for n, piece in enumerate((high, low, rest)):
                xl_ref[64 * n + 32 * k : 64 * n + 32 * k + 32, tile_of(p)] = piece
    degrees = slots_ref[...]
    for t in range(8):
        d = degrees[t : t + 1, :]
        where_from = (d % 6) * LANES + d // 6
        pick = jnp.where(row_index((LDEG, LANES)) == where_from, 1.0, 0.0).astype(bf16)
        chosen = mm(xl_ref[0:192, 0:LDEG], pick)
        chosen = chosen[0:64] + chosen[64:128] + chosen[128:192]
        for k in range(4):
            stage_ref[pl.ds(LANES * k + t, 16, stride=8), :] = chosen[16 * k : 16 * k + 16]
    for k in range(4):
        send_ref[:, tile_of(k)] = stage_ref[tile_of(k), :]

    high, low = split(jnp.concatenate([coef_ref[0:192, :], coef_ref[256:448, :]], 1))
    field = mm(high, th_ref[...]) + mm(low, th_ref[...]) + mm(high, tl_ref[...])
    re, im = [], []
    for p in range(6):
        cosine, sine = twiddle_ref[0, p : p + 1, :], twiddle_ref[1, p : p + 1, :]
        x, y = field[32 * p : 32 * p + 32, 0:256], field[32 * p : 32 * p + 32, 256:512]
        re.append(x * cosine - y * sine)
        im.append(x * sine + y * cosine)
    a1, a2, e1, e2 = re[1] + re[5], re[2] + re[4], im[1] - im[5], im[2] - im[4]
    plus, minus = re[0] + re[3], re[0] - re[3]
    half, diff = 0.5 * (a1 + a2), 0.5 * (a1 - a2)
    o1, o2 = ROOT3H * (e1 + e2), ROOT3H * (e1 - e2)
    parts = [plus + 2.0 * half, minus + diff - o1, plus - half - o2, minus - 2.0 * diff,
             plus - half + o2, minus + diff + o1]
    for a in range(6):
        basis_ref[0, 0:32, 256 * a : 256 * a + 256] += gravity_gain * density * parts[a]

    idx = row_index((32, LANES))
    lane32 = lane_index((32, LANES))
    after = jnp.where(idx < 16, idx + 16, jnp.where(idx == 31, -1000, idx - 15))
    before = jnp.where(idx >= 16, idx - 16, jnp.where(idx == 0, -1000, idx + 15))
    masks = {}
    for c in range(3):
        for name, index in ((0, idx), (1, after), (-1, before)):
            masks[c, name] = jnp.where(lane32 == index + 32 * c, 1.0, 0.0)
    for g in range(2):
        for n in range(2):
            for c in range(3):
                row = 4 * c + 2 * n + g
                start = 96 * n + 32 * c
                for dh in range(2):
                    block = jnp.zeros((32, LANES), f32)
                    for c2 in range(3):
                        for dr in range(2):
                            value = stiff_ref[12 * row + 4 * c2 + 2 * dr + dh]
                            block = block + value * masks[c2, dr - n]
                    high, low = split(block)
                    matrix_ref[g, start : start + 32, tile_of(dh)] = high
                    matrix_ref[g, 192 + start : 224 + start, tile_of(dh)] = low

    for k in range(3):
        pad = jnp.zeros((32, HRING), bf16)
        xh_ref[128 * k + 96 : 128 * k + 128, :] = pad
        xl_ref[128 * k + 96 : 128 * k + 128, :] = pad

    lane_row = lane_index((1, LANES))

    def step(j, state):
        moments, beta = state
        v = basis_ref[j + 1]
        for k, x in ((0, pltpu.roll(v, 1, 1)), (128, v), (256, pltpu.roll(v, HRING - 1, 1))):
            high, low = split(x)
            xh_ref[k : k + 96, :] = high
            xl_ref[k : k + 96, :] = low
        product = jnp.zeros((96, 256), f32)
        for n in range(6):
            cols = slice(256 * n, 256 * n + 256)
            total = None
            for g in range(2):
                rows = slice(128 * (1 - g), 128 * (1 - g) + 256)
                first = mm(matrix_ref[g], xh_ref[rows, cols])
                second = mm(matrix_ref[g, 0:192, :], xl_ref[rows, cols])
                force = first[0:192] + first[192:384] + second
                for i in range(2):
                    share = eff_ref[2 * g + i, :, cols]
                    term = force[96 * i : 96 * i + 96].reshape(3, 32, 256) * share[None]
                    total = term if total is None else total + term
            total = total.reshape(96, 256)
            image_ref[:, cols] = total
            product = product + total * basis_ref[j + 1, :, cols]
        inner = jnp.sum(jnp.sum(product, 0, keepdims=True), 1, keepdims=True)
        alpha = jnp.where(j == 0, 0.0, inner)
        moments = moments + jnp.where(lane_row == j - 1, alpha, 0.0)
        rest = image_ref[...] - alpha * basis_ref[j + 1] - beta * basis_ref[j]
        norm2 = jnp.sum(jnp.sum(rest * rest, 0, keepdims=True), 1, keepdims=True)
        inverse = jnp.where(norm2 > 0.0, lax.rsqrt(norm2), 0.0)
        norm = norm2 * inverse

        @pl.when(j < 6)
        def _():
            basis_ref[j + 2] = rest * jnp.where(j == 0, -inverse, inverse)

        slot = jnp.where(j == 0, 16, jnp.where(j < 6, 7 + j, 100))
        moments = moments + jnp.where(lane_row == slot, norm, 0.0)
        return moments, jnp.where(j == 0, 0.0, norm)

    moments, _ = lax.fori_loop(
        0, 7, step, (jnp.zeros((1, LANES), f32), jnp.ones((1, 1), f32))
    )
    send_ref[:, tile_of(4)] = jnp.broadcast_to(moments, (LANES, LANES))


def solve_kernel(place_ref, moments_ref, basis_ref, out_ref, x_ref, stage_ref):
    table = jnp.transpose(moments_ref[...])
    diagonal, beside, start = table[0:8], table[8:16], table[16:17]
    first = row_index((8, LANES)) == 0
    residual = jnp.where(first, start, 0.0)

    def total(x):
        return jnp.sum(jnp.sum(x, 0, keepdims=True), 1, keepdims=True)

    direction, y = residual, jnp.zeros((8, LANES), f32)
    rr = total(residual * residual)
    for i in range(6):
        image = (
            diagonal * direction
            + beside * pltpu.roll(direction, 7, 0)
            + pltpu.roll(beside * direction, 1, 0)
        )
        size = rr / total(direction * image)
        y = y + size * direction
        if i < 5:
            residual = residual - size * image
            new = total(residual * residual)
            direction = residual + (new / rr) * direction
            rr = new
    mine = lane_index((8, LANES)) == place_ref[0]
    own = jnp.sum(jnp.where(mine, y, 0.0), 1, keepdims=True)
    x = basis_ref[1]
    for i in range(6):
        x = x + own[i : i + 1, :] * basis_ref[2 + i]
    x_ref[...] = x

    lane = lane_index((16, LANES))

    def node_rows(c, r, k):
        block = x_ref[32 * c + 16 * (r % 2) : 32 * c + 16 * (r % 2) + 16, tile_of(k)]
        return up_one(block) if r == 2 else block

    def at(t, tile):
        return pl.ds(LANES * tile + t, 16, stride=8)

    for u in range(4):
        even, odd = 2 * u, 2 * u + 1
        for c in range(3):
            for r in range(3):
                stage_ref[at(even, 4 * c + r), :] = node_rows(c, r, 3 * u)
                stage_ref[at(odd, 4 * c + r), :] = node_rows(c, r, 3 * u + 2)
            low, high = node_rows(c, 0, 3 * u + 1), node_rows(c, 1, 3 * u + 1)
            stage_ref[at(even, 4 * c + 3), :] = jnp.where(lane < 64, low, pltpu.roll(high, 64, 1))
            stage_ref[at(odd, 4 * c + 3), :] = jnp.where(lane < 64, pltpu.roll(low, 64, 1), high)
        extra = [node_rows(c, 2, 3 * u + 1) for c in range(3)]
        stage_ref[at(even, OUT_TAIL), :] = jnp.where(
            lane < 64, extra[0], pltpu.roll(extra[1], 64, 1)
        )
        stage_ref[at(odd, OUT_TAIL), :] = jnp.where(
            lane < 64, pltpu.roll(extra[0], 64, 1), extra[1]
        )
        for parity, rows in ((0, even), (1, odd)):
            block = extra[2] if parity == 0 else pltpu.roll(extra[2], 64, 1)
            following = (2 * u + parity + 1) % 8
            k, source = 3 * (following // 2) + following % 2, 64 * (following % 2)
            for c in range(3):
                for r in range(3):
                    target = 64 + 3 * c + r
                    value = pltpu.roll(node_rows(c, r, k), (target - source) % LANES, 1)
                    block = jnp.where(lane == target, value, block)
            stage_ref[at(rows, OUT_TAIL + 1), :] = block
    for k in range(OUT_TILES):
        out_ref[:, tile_of(k)] = stage_ref[tile_of(k), :]


def finish_kernel(parity_ref, stiff_ref, recv_ref, stress_ref, shear_ref, relax_ref,
                  x_out_ref, stress_out_ref, x_ref, eff_ref, kept_ref):
    comp = pl.program_id(0)
    parity = parity_ref[0]
    wide = pl.ds(pl.multiple_of(64 * parity, 64), 128)
    narrow = pl.ds(pl.multiple_of(128 * (1 - parity), 64), 64)

    @pl.when(comp == 0)
    def _():
        relax = relax_ref[...]
        share = 1.0 / (1.0 + 0.5 * relax)
        eff_ref[...] = shear_ref[...] * share
        kept_ref[...] = (1.0 - 0.5 * relax) * share
        def block(k):
            return jnp.transpose(recv_ref[:, tile_of(k)])
        for c in range(3):
            for r in range(3):
                x_ref[c, r, wide, :] = block(4 * c + r)
            rest = block(4 * c + 3)
            x_ref[c, 0, narrow, :] = rest[0:64]
            x_ref[c, 1, narrow, :] = rest[64:128]
        rest = block(OUT_TAIL)
        x_ref[0, 2, narrow, :] = rest[0:64]
        x_ref[1, 2, narrow, :] = rest[64:128]
        rest = block(OUT_TAIL + 1)
        x_ref[2, 2, narrow, :] = rest[0:64]
        for c in range(3):
            for r in range(3):
                x_ref[c, r, COLS : COLS + 1, :] = rest[64 + 3 * c + r : 65 + 3 * c + r]
        for c in range(3):
            x_out_ref[c] = x_ref[c, 0:2, 0:COLS, :]

    chunk = 24
    for r in range(2):
        for n in range(COLS // chunk):
            start = n * chunk
            rows = slice(start, start + chunk)
            corners = []
            for c in range(3):
                for dr in range(2):
                    for dh in range(2):
                        corners.append(x_ref[c, r + dr, start + dh : start + dh + chunk, :])
            eff, kept = eff_ref[r, rows, :], kept_ref[r, rows, :]
            for q in range(4):
                row = (4 * comp + q) * 12
                force = stiff_ref[row] * corners[0]
                for k in range(1, 12):
                    force = force + stiff_ref[row + k] * corners[k]
                stress_out_ref[q, r, rows, :] = kept * stress_ref[q, r, rows, :] + eff * force


def potential_kernel(recv_ref, out_ref):
    for part in range(2):
        for r in range(2):
            block = jnp.transpose(recv_ref[:, tile_of(2 * part + r)])
            out_ref[:, r, tile_of(part)] = block[0:96]


def whole(shape):
    return pl.BlockSpec(shape, lambda *_: (0,) * len(shape))


smem = pl.BlockSpec(memory_space=pltpu.SMEM)


def params(mib):
    return pltpu.CompilerParams(vmem_limit_bytes=mib * 2**20)


def body(load, previous, stress_old, shear_modulus, relaxation, density_jump, element_stiffness,
         degree_slots):
    tile_place = lax.axis_index(TILE)
    place = (lax.axis_index(CAP) * 8 + tile_place).astype(jnp.int32).reshape(1)
    parity = (tile_place % 2).astype(jnp.int32).reshape(1)
    stiff = element_stiffness.reshape(144)
    slots = jnp.pad(degree_slots.reshape(8, 96), ((0, 0), (0, 32)), constant_values=-1)
    (fh, fl), (th, tl), twiddle = transform_tables()
    ratio, scale, radius = radial_tables()

    one = pl.BlockSpec((1, 2, COLS, LANES), lambda c: (c, 0, 0, 0))
    four = pl.BlockSpec((4, 2, COLS, LANES), lambda c: (c, 0, 0, 0))
    field = whole((2, COLS, LANES))
    packed = pl.pallas_call(
        pack_kernel,
        grid=(3,),
        in_specs=[smem, smem, one, one, four, field, field],
        out_specs=whole((LANES, IN_TILES * LANES)),
        out_shape=jax.ShapeDtypeStruct((LANES, IN_TILES * LANES), f32),
        scratch_shapes=[pltpu.VMEM((3, COLS, LANES), f32), pltpu.VMEM((256, LANES), f32)],
        compiler_params=params(24),
    )(parity, density_jump, load, previous, stress_old, shear_modulus, relaxation)
    received = lax.all_to_all(packed, ALL, 0, 0, tiled=True)

    basis, sent = pl.pallas_call(
        functools.partial(section_kernel, radius=[float(x) for x in radius]),
        in_specs=[smem] + [pl.BlockSpec(memory_space=pltpu.VMEM)] * 9,
        out_specs=[pl.BlockSpec(memory_space=pltpu.VMEM)] * 2,
        out_shape=[
            jax.ShapeDtypeStruct((8, 96, HRING), f32),
            jax.ShapeDtypeStruct((LANES, 5 * LANES), f32),
        ],
        scratch_shapes=[
            pltpu.VMEM((4, 32, HRING), f32),
            pltpu.VMEM((2, 384, 256), bf16),
            pltpu.VMEM((384, HRING), bf16),
            pltpu.VMEM((384, HRING), bf16),
            pltpu.VMEM((96, HRING), f32),
            pltpu.VMEM((512, LANES), f32),
            pltpu.VMEM((NR, 8, 256), f32),
            pltpu.VMEM((IN_TILES * LANES, LANES), f32),
        ],
        compiler_params=params(48),
    )(stiff, received, slots, fh, fl, th, tl, twiddle, ratio, scale)
    shared = lax.all_to_all(sent, ALL, 0, 0, tiled=True)

    back = pl.pallas_call(
        solve_kernel,
        grid=(1,),
        in_specs=[
            smem,
            pl.BlockSpec((LANES, LANES), lambda i: (0, 4)),
            whole((8, 96, HRING)),
        ],
        out_specs=whole((LANES, OUT_TILES * LANES)),
        out_shape=jax.ShapeDtypeStruct((LANES, OUT_TILES * LANES), f32),
        scratch_shapes=[
            pltpu.VMEM((96, HRING), f32),
            pltpu.VMEM((OUT_TILES * LANES, LANES), f32),
        ],
        compiler_params=params(32),
    )(place, shared, basis)
    returned = lax.all_to_all(back, ALL, 0, 0, tiled=True)

    potential = pl.pallas_call(
        potential_kernel,
        grid=(1,),
        in_specs=[pl.BlockSpec((LANES, 4 * LANES), lambda i: (0, 0))],
        out_specs=whole((96, 2, 256)),
        out_shape=jax.ShapeDtypeStruct((96, 2, 256), f32),
        compiler_params=params(16),
    )(shared)

    displacement, stress_new = pl.pallas_call(
        finish_kernel,
        grid=(3,),
        in_specs=[smem, smem, whole((LANES, OUT_TILES * LANES)), four, field, field],
        out_specs=[whole((3, 2, COLS, LANES)), four],
        out_shape=[
            jax.ShapeDtypeStruct((3, 2, COLS, LANES), f32),
            jax.ShapeDtypeStruct((12, 2, COLS, LANES), f32),
        ],
        scratch_shapes=[
            pltpu.VMEM((3, 3, COLS + 8, LANES), f32),
            pltpu.VMEM((2, COLS, LANES), f32),
            pltpu.VMEM((2, COLS, LANES), f32),
        ],
        compiler_params=params(24),
    )(parity, stiff, returned, stress_old, shear_modulus, relaxation)
    return displacement, stress_new, potential


def solution(mesh):
    torus = Mesh(mesh.devices.reshape(4, 4, 4, 2), ("cap_0", "cap_1", "tile_0", "tile_1"))
    return jax.shard_map(
        body,
        mesh=torus,
        in_specs=(
            P(None, CAP, TILE, None),
            P(None, CAP, TILE, None),
            P(None, CAP, TILE, None),
            P(CAP, TILE, None),
            P(CAP, TILE, None),
            P(CAP),
            P(),
            P(),
        ),
        out_specs=(P(None, CAP, TILE, None), P(None, CAP, TILE, None), P(TILE, CAP, None)),
        check_vma=False,
    )
```

```python
import functools
import math

import jax
import jax.numpy as jnp
import ml_dtypes
import numpy as np
from jax import lax
from jax.experimental import pallas as pl
from jax.experimental.pallas import tpu as pltpu
from jax.sharding import Mesh
from jax.sharding import PartitionSpec as P

HRING = 1536
LDEG = 768
NR = 32
TILE = ("tile_0", "tile_1")
CAP = ("cap_0", "cap_1")
ALL = ("cap_0", "cap_1", "tile_0", "tile_1")
LANES = 128
COLS = 192
ROOT3H = math.sqrt(3.0) / 2.0
rotation_gain = 2.0
gravity_gain = 0.2

EFF_TILE = 21
TAIL_TILE = 24
IN_TILES = 26
MID_TILES = 4
OUT_TAIL = 12
OUT_TILES = 14

f32 = jnp.float32
bf16 = jnp.bfloat16


def split_table(table):
    high = table.astype(ml_dtypes.bfloat16)
    low = (table - high.astype(np.float64)).astype(ml_dtypes.bfloat16)
    return high, low


def transform_tables():
    q = np.arange(128)[None, :]
    b = np.arange(256)[:, None]
    angle = 2.0 * np.pi * ((q * b) % 256) / 256.0
    cosine, sine = np.cos(angle), np.sin(angle)
    table = np.concatenate(
        [np.concatenate([cosine, sine], 1), np.concatenate([sine, -cosine], 1)], 0
    )
    p = np.arange(8)[:, None]
    turn = 2.0 * np.pi * ((p * np.arange(256)[None, :]) % HRING) / HRING
    twiddle = np.stack([np.cos(turn), np.sin(turn)]).astype(np.float32)
    return split_table(table), split_table(np.ascontiguousarray(table.T)), twiddle


def radial_tables():
    radius = 1.0 - 0.45 * (np.arange(NR) + 0.5) / NR
    degree = 6.0 * np.arange(128)[None, :] + np.arange(8)[:, None]
    log_radius = np.log(radius)
    ratio = np.zeros((NR, 8, 128))
    for r in range(1, NR):
        ratio[r] = np.exp(-degree * (log_radius[r - 1] - log_radius[r]))
    scale = 1.0 / np.sqrt(2.0 * degree + 1.0)
    return ratio.astype(np.float32), scale.astype(np.float32), radius


def split(x):
    high = x.astype(bf16)
    return high, (x - high.astype(f32)).astype(bf16)


def mm(a, b):
    return jnp.dot(a, b, preferred_element_type=f32)


def lane_index(shape):
    return lax.broadcasted_iota(jnp.int32, shape, len(shape) - 1)


def row_index(shape):
    return lax.broadcasted_iota(jnp.int32, shape, 0)


def tile_of(k):
    return slice(k * LANES, (k + 1) * LANES)


def down_one(x):
    return jnp.where(row_index(x.shape) == 0, 0.0, pltpu.roll(x, 1, 0))


def up_one(x):
    n = x.shape[0]
    return jnp.where(row_index(x.shape) == n - 1, 0.0, pltpu.roll(x, n - 1, 0))


def pack_kernel(parity_ref, density_ref, load_ref, prev_ref, stress_ref, shear_ref, relax_ref,
                out_ref, acc_ref, tail_ref):
    comp = pl.program_id(0)
    parity = parity_ref[0]
    wide = pl.ds(pl.multiple_of(64 * parity, 64), 128)
    narrow = pl.ds(pl.multiple_of(128 * (1 - parity), 64), 64)

    def put(tile, block):
        out_ref[pl.ds(tile, LANES, stride=IN_TILES), :] = jnp.transpose(block)

    @pl.when(comp == 0)
    def _():
        acc_ref[:2] = shear_ref[...] / (1.0 + 0.5 * relax_ref[...])
        put(EFF_TILE, acc_ref[0, wide, :])
        put(EFF_TILE + 1, acc_ref[1, wide, :])
        put(EFF_TILE + 2, jnp.concatenate([acc_ref[0, narrow, :], acc_ref[1, narrow, :]], 0))
        tail_ref[192:256, :] = jnp.zeros((64, LANES), f32)
        for r in range(2):
            tail_ref[201 + r : 202 + r, :] = jnp.full((1, LANES), density_ref[r], f32)

    base = comp * 7
    put(base, prev_ref[0, 0, wide, :])
    put(base + 1, prev_ref[0, 1, wide, :])
    put(base + 2, jnp.concatenate([prev_ref[0, 0, narrow, :], prev_ref[0, 1, narrow, :]], 0))

    relax = relax_ref[...]
    carried = relax / (1.0 + 0.5 * relax)
    part = [[carried[r] * stress_ref[q, r] for r in range(2)] for q in range(4)]
    near = [part[0][0], part[0][1] + part[2][0], part[2][1]]
    far = [part[1][0], part[1][1] + part[3][0], part[3][1]]
    for r in range(3):
        total = near[r] + down_one(far[r])
        if r < 2:
            total = total + load_ref[0, r]
        acc_ref[r] = total
        tail_ref[pl.ds(192 + 3 * comp + r, 1), :] = far[r][COLS - 1 : COLS, :]
    for r in range(3):
        put(base + 3 + r, acc_ref[r, wide, :])
    put(base + 6, jnp.concatenate([acc_ref[0, narrow, :], acc_ref[1, narrow, :]], 0))
    tail_ref[pl.ds(pl.multiple_of(64 * comp, 64), 64), :] = acc_ref[2, narrow, :]

    @pl.when(comp == 2)
    def _():
        put(TAIL_TILE, tail_ref[:128, :])
        put(TAIL_TILE + 1, tail_ref[128:, :])


def section_kernel(stiff_ref, recv_ref, slots_ref, fh_ref, fl_ref, th_ref, tl_ref, twiddle_ref,
                   ratio_ref, scale_ref, kept_ref, send_ref, basis_ref, sems,
                   eff_ref, matrix_ref, xh_ref, xl_ref, image_ref, coef_ref, pot_ref,
                   *, radius):
    lane = lane_index((16, LANES))

    def leaving(slot):
        return pltpu.make_async_copy(basis_ref.at[slot + 1], kept_ref.at[slot], sems.at[slot])

    def rows_of(t, tile):
        return recv_ref[pl.ds(IN_TILES * t + tile, 16, stride=8 * IN_TILES), :]

    def unrolled(wide_tile, narrow_tile, half):
        for u in range(4):
            even, odd = rows_of(2 * u, narrow_tile), rows_of(2 * u + 1, narrow_tile)
            if half == 0:
                middle = jnp.where(lane < 64, even, pltpu.roll(odd, 64, 1))
            else:
                middle = jnp.where(lane < 64, pltpu.roll(even, 64, 1), odd)
            yield 3 * u, rows_of(2 * u, wide_tile)
            yield 3 * u + 1, middle
            yield 3 * u + 2, rows_of(2 * u + 1, wide_tile)

    tail = TAIL_TILE
    for c in range(3):
        for r in range(2):
            rows = slice(32 * c + 16 * r, 32 * c + 16 * r + 16)
            for k, block in unrolled(7 * c + r, 7 * c + 2, r):
                basis_ref[1, rows, tile_of(k)] = block
            for k, block in unrolled(7 * c + 3 + r, 7 * c + 6, r):
                basis_ref[0, rows, tile_of(k)] = block
        rows = slice(32 * c, 32 * c + 16)
        for k, block in unrolled(7 * c + 5, tail + c // 2, c % 2):
            basis_ref[0, rows, tile_of(k)] += down_one(block)
    leaving(0).start()
    for t in range(8):
        following = (t + 1) % 8
        k, target = 3 * (following // 2) + following % 2, 64 * (following % 2)
        block = rows_of(t, tail + 1)
        for c in range(3):
            for r in range(3):
                shift = (target - 64 - 3 * c - r) % LANES
                value = jnp.where(lane == target, pltpu.roll(block, shift, 1), 0.0)
                if r == 2:
                    value = down_one(value)
                start = 32 * c + 16 * (r % 2)
                basis_ref[0, start : start + 16, tile_of(k)] += value
    for r in range(2):
        for k, block in unrolled(EFF_TILE + r, EFF_TILE + 2, r):
            eff_ref[0, 16 * r : 16 * r + 16, tile_of(k)] = block
    eff_ref[1, 16:32, :] = eff_ref[0, 0:16, :]
    eff_ref[1, 0:16, :] = down_one(eff_ref[0, 16:32, :])
    eff_ref[2] = pltpu.roll(eff_ref[0], 1, 1)
    eff_ref[3] = pltpu.roll(eff_ref[1], 1, 1)

    density = jnp.concatenate(
        [jnp.sum(jnp.where(lane == 73 + r, rows_of(0, tail + 1), 0.0), 1, keepdims=True)
         for r in range(2)], 0
    )

    weight = density * math.sqrt(2.0 / HRING)
    w = [basis_ref[1, 0:32, 256 * a : 256 * a + 256] * weight for a in range(6)]
    s1, s2, d1, d2 = w[1] + w[5], w[2] + w[4], w[1] - w[5], w[2] - w[4]
    plus, minus = w[0] + w[3], w[0] - w[3]
    half = 0.5 * (s1 + s2)
    diff = 0.5 * (s1 - s2)
    real = [plus + 2.0 * half, minus + diff, plus - half, minus - 2.0 * diff]
    real += [real[2], real[1]]
    i1, i2 = -ROOT3H * (d1 + d2), -ROOT3H * (d1 - d2)
    imag = [None, i1, i2, None, -i2, -i1]
    for p in range(6):
        cosine, sine = twiddle_ref[0, p : p + 1, :], twiddle_ref[1, p : p + 1, :]
        rows = slice(32 * p, 32 * p + 32)
        re, im = real[p] * cosine, -real[p] * sine
        if imag[p] is not None:
            re, im = re + imag[p] * sine, im + imag[p] * cosine
        for k, x in ((0, re), (256, im)):
            high, low = split(x)
            xh_ref[rows, k : k + 256] = high
            xl_ref[rows, k : k + 256] = low
    high, low = xh_ref[0:192, 0:512], xl_ref[0:192, 0:512]
    coefs = mm(high, fh_ref[...]) + mm(low, fh_ref[...]) + mm(high, fl_ref[...])
    for k in range(2):
        coef_ref[256 * k : 256 * k + 192, :] = coefs[:, tile_of(k)]
        coef_ref[256 * k + 192 : 256 * k + 256, :] = jnp.zeros((64, LANES), f32)

    def place(r, k):
        return pl.ds(256 * k + 16 * (r % 2) + r // 2, 8, stride=32)

    zero = jnp.zeros((8, LANES), f32)
    for k in range(2):
        lanes = tile_of(k)
        rows = [coef_ref[place(r, k), :] for r in range(NR)]
        forward, moment = zero, zero
        for r in range(NR):
            forward = rows[r] + ratio_ref[r] * forward
            moment = moment + (radius[r] ** 4 / NR) * rows[r]
            pot_ref[r, :, lanes] = forward
        chosen = (lane_index((8, LANES)) == 0) & (row_index((8, LANES)) == 2)
        moment = jnp.where(chosen, rotation_gain * moment, 0.0)
        back = zero
        for r in reversed(range(NR)):
            if r + 1 < NR:
                back = ratio_ref[r + 1] * (rows[r + 1] + back)
            pot_ref[r, :, lanes] = (
                (pot_ref[r, :, lanes] + back) * scale_ref[...] + radius[r] ** 2 * moment
            )
    for k in range(2):
        for r in range(NR):
            coef_ref[place(r, k), :] = pot_ref[r, :, tile_of(k)]

    for k in range(2):
        for p in range(6):
            x = coef_ref[256 * k + 32 * p : 256 * k + 32 * p + 32, :]
            high, low = split(x)
            rest = (x - high.astype(f32) - low.astype(f32)).astype(bf16)
            for n, piece in enumerate((high, low, rest)):
                xl_ref[64 * n + 32 * k : 64 * n + 32 * k + 32, tile_of(p)] = piece
    degrees = slots_ref[...]
    for t in range(8):
        d = degrees[t : t + 1, :]
        where_from = (d % 6) * LANES + d // 6
        pick = jnp.where(row_index((LDEG, LANES)) == where_from, 1.0, 0.0).astype(bf16)
        chosen = mm(xl_ref[0:192, 0:LDEG], pick)
        chosen = chosen[0:64] + chosen[64:128] + chosen[128:192]
        c0, c1, c2, c3 = [chosen[16 * k : 16 * k + 16] for k in range(4)]
        joined = [
            jnp.where(lane < 96, c0, pltpu.roll(c1, 96, 1)),
            jnp.where(lane < 64, pltpu.roll(c1, 96, 1), pltpu.roll(c2, 64, 1)),
            jnp.where(lane < 32, pltpu.roll(c2, 64, 1), pltpu.roll(c3, 32, 1)),
        ]
        for k, block in enumerate(joined):
            send_ref[pl.ds(MID_TILES * t + k, 16, stride=8 * MID_TILES), :] = block

    high, low = split(jnp.concatenate([coef_ref[0:192, :], coef_ref[256:448, :]], 1))
    field = mm(high, th_ref[...]) + mm(low, th_ref[...]) + mm(high, tl_ref[...])
    re, im = [], []
    for p in range(6):
        cosine, sine = twiddle_ref[0, p : p + 1, :], twiddle_ref[1, p : p + 1, :]
        x, y = field[32 * p : 32 * p + 32, 0:256], field[32 * p : 32 * p + 32, 256:512]
        re.append(x * cosine - y * sine)
        im.append(x * sine + y * cosine)
    a1, a2, e1, e2 = re[1] + re[5], re[2] + re[4], im[1] - im[5], im[2] - im[4]
    plus, minus = re[0] + re[3], re[0] - re[3]
    half, diff = 0.5 * (a1 + a2), 0.5 * (a1 - a2)
    o1, o2 = ROOT3H * (e1 + e2), ROOT3H * (e1 - e2)
    parts = [plus + 2.0 * half, minus + diff - o1, plus - half - o2, minus - 2.0 * diff,
             plus - half + o2, minus + diff + o1]
    for a in range(6):
        basis_ref[0, 0:32, 256 * a : 256 * a + 256] += gravity_gain * density * parts[a]

    idx = row_index((32, LANES))
    lane32 = lane_index((32, LANES))
    after = jnp.where(idx < 16, idx + 16, jnp.where(idx == 31, -1000, idx - 15))
    before = jnp.where(idx >= 16, idx - 16, jnp.where(idx == 0, -1000, idx + 15))
    masks = {}
    for c in range(3):
        for name, index in ((0, idx), (1, after), (-1, before)):
            masks[c, name] = jnp.where(lane32 == index + 32 * c, 1.0, 0.0)
    for g in range(2):
        for n in range(2):
            for c in range(3):
                row = 4 * c + 2 * n + g
                start = 96 * n + 32 * c
                for dh in range(2):
                    block = jnp.zeros((32, LANES), f32)
                    for c2 in range(3):
                        for dr in range(2):
                            value = stiff_ref[12 * row + 4 * c2 + 2 * dr + dh]
                            block = block + value * masks[c2, dr - n]
                    high, low = split(block)
                    matrix_ref[g, start : start + 32, tile_of(dh)] = high
                    matrix_ref[g, 192 + start : 224 + start, tile_of(dh)] = low

    for k in range(3):
        pad = jnp.zeros((32, HRING), bf16)
        xh_ref[128 * k + 96 : 128 * k + 128, :] = pad
        xl_ref[128 * k + 96 : 128 * k + 128, :] = pad

    lane_row = lane_index((1, LANES))

    def step(j, state):
        moments, beta = state
        v = basis_ref[j + 1]
        for k, x in ((0, pltpu.roll(v, 1, 1)), (128, v), (256, pltpu.roll(v, HRING - 1, 1))):
            high, low = split(x)
            xh_ref[k : k + 96, :] = high
            xl_ref[k : k + 96, :] = low
        product = jnp.zeros((96, 256), f32)
        for n in range(6):
            cols = slice(256 * n, 256 * n + 256)
            total = None
            for g in range(2):
                rows = slice(128 * (1 - g), 128 * (1 - g) + 256)
                first = mm(matrix_ref[g], xh_ref[rows, cols])
                second = mm(matrix_ref[g, 0:192, :], xl_ref[rows, cols])
                force = first[0:192] + first[192:384] + second
                for i in range(2):
                    share = eff_ref[2 * g + i, :, cols]
                    term = force[96 * i : 96 * i + 96].reshape(3, 32, 256) * share[None]
                    total = term if total is None else total + term
            total = total.reshape(96, 256)
            image_ref[:, cols] = total
            product = product + total * basis_ref[j + 1, :, cols]
        inner = jnp.sum(jnp.sum(product, 0, keepdims=True), 1, keepdims=True)
        alpha = jnp.where(j == 0, 0.0, inner)
        moments = moments + jnp.where(lane_row == j - 1, alpha, 0.0)
        rest = image_ref[...] - alpha * basis_ref[j + 1] - beta * basis_ref[j]
        norm2 = jnp.sum(jnp.sum(rest * rest, 0, keepdims=True), 1, keepdims=True)
        inverse = jnp.where(norm2 > 0.0, lax.rsqrt(norm2), 0.0)
        norm = norm2 * inverse

        @pl.when(j < 6)
        def _():
            basis_ref[j + 2] = rest * jnp.where(j == 0, -inverse, inverse)
            leaving(j + 1).start()

        slot = jnp.where(j == 0, 16, jnp.where(j < 6, 7 + j, 100))
        moments = moments + jnp.where(lane_row == slot, norm, 0.0)
        return moments, jnp.where(j == 0, 0.0, norm)

    moments, _ = lax.fori_loop(
        0, 7, step, (jnp.zeros((1, LANES), f32), jnp.ones((1, 1), f32))
    )
    send_ref[pl.ds(3, LANES, stride=MID_TILES), :] = jnp.broadcast_to(moments, (LANES, LANES))
    for slot in range(7):
        leaving(slot).wait()


def solve_kernel(place_ref, moments_ref, kept_ref, out_ref, x_ref, basis_ref, sems):
    def arriving(slot):
        return pltpu.make_async_copy(kept_ref.at[slot], basis_ref.at[slot], sems.at[slot])

    for slot in range(7):
        arriving(slot).start()
    table = jnp.transpose(moments_ref[pl.ds(3, LANES, stride=MID_TILES), :])
    diagonal, beside, start = table[0:8], table[8:16], table[16:17]
    first = row_index((8, LANES)) == 0
    residual = jnp.where(first, start, 0.0)

    def total(x):
        return jnp.sum(jnp.sum(x, 0, keepdims=True), 1, keepdims=True)

    direction, y = residual, jnp.zeros((8, LANES), f32)
    rr = total(residual * residual)
    for i in range(6):
        image = (
            diagonal * direction
            + beside * pltpu.roll(direction, 7, 0)
            + pltpu.roll(beside * direction, 1, 0)
        )
        size = rr / total(direction * image)
        y = y + size * direction
        if i < 5:
            residual = residual - size * image
            new = total(residual * residual)
            direction = residual + (new / rr) * direction
            rr = new
    mine = lane_index((8, LANES)) == place_ref[0]
    own = jnp.sum(jnp.where(mine, y, 0.0), 1, keepdims=True)
    for slot in range(7):
        arriving(slot).wait()
    x = basis_ref[0]
    for i in range(6):
        x = x + own[i : i + 1, :] * basis_ref[1 + i]
    x_ref[...] = x

    lane = lane_index((16, LANES))

    def node_rows(c, r, k):
        block = x_ref[32 * c + 16 * (r % 2) : 32 * c + 16 * (r % 2) + 16, tile_of(k)]
        return up_one(block) if r == 2 else block

    def at(t, tile):
        return pl.ds(OUT_TILES * t + tile, 16, stride=8 * OUT_TILES)

    for u in range(4):
        even, odd = 2 * u, 2 * u + 1
        for c in range(3):
            for r in range(3):
                out_ref[at(even, 4 * c + r), :] = node_rows(c, r, 3 * u)
                out_ref[at(odd, 4 * c + r), :] = node_rows(c, r, 3 * u + 2)
            low, high = node_rows(c, 0, 3 * u + 1), node_rows(c, 1, 3 * u + 1)
            out_ref[at(even, 4 * c + 3), :] = jnp.where(lane < 64, low, pltpu.roll(high, 64, 1))
            out_ref[at(odd, 4 * c + 3), :] = jnp.where(lane < 64, pltpu.roll(low, 64, 1), high)
        extra = [node_rows(c, 2, 3 * u + 1) for c in range(3)]
        out_ref[at(even, OUT_TAIL), :] = jnp.where(
            lane < 64, extra[0], pltpu.roll(extra[1], 64, 1)
        )
        out_ref[at(odd, OUT_TAIL), :] = jnp.where(
            lane < 64, pltpu.roll(extra[0], 64, 1), extra[1]
        )
        for parity, rows in ((0, even), (1, odd)):
            block = extra[2] if parity == 0 else pltpu.roll(extra[2], 64, 1)
            following = (2 * u + parity + 1) % 8
            k, source = 3 * (following // 2) + following % 2, 64 * (following % 2)
            for c in range(3):
                for r in range(3):
                    target = 64 + 3 * c + r
                    value = pltpu.roll(node_rows(c, r, k), (target - source) % LANES, 1)
                    block = jnp.where(lane == target, value, block)
            out_ref[at(rows, OUT_TAIL + 1), :] = block


def finish_kernel(parity_ref, stiff_ref, recv_ref, stress_ref, eff_ref, kept_ref,
                  x_out_ref, stress_out_ref, x_ref):
    comp = pl.program_id(0)
    parity = parity_ref[0]
    wide = pl.ds(pl.multiple_of(64 * parity, 64), 128)
    narrow = pl.ds(pl.multiple_of(128 * (1 - parity), 64), 64)

    @pl.when(comp == 0)
    def _():
        def block(k):
            return jnp.transpose(recv_ref[pl.ds(k, LANES, stride=OUT_TILES), :])
        for c in range(3):
            for r in range(3):
                x_ref[c, r, wide, :] = block(4 * c + r)
            rest = block(4 * c + 3)
            x_ref[c, 0, narrow, :] = rest[0:64]
            x_ref[c, 1, narrow, :] = rest[64:128]
        rest = block(OUT_TAIL)
        x_ref[0, 2, narrow, :] = rest[0:64]
        x_ref[1, 2, narrow, :] = rest[64:128]
        rest = block(OUT_TAIL + 1)
        x_ref[2, 2, narrow, :] = rest[0:64]
        for c in range(3):
            for r in range(3):
                x_ref[c, r, COLS : COLS + 1, :] = rest[64 + 3 * c + r : 65 + 3 * c + r]
        for c in range(3):
            x_out_ref[c] = x_ref[c, 0:2, 0:COLS, :]

    chunk = 24
    for r in range(2):
        for n in range(COLS // chunk):
            start = n * chunk
            rows = slice(start, start + chunk)
            corners = []
            for c in range(3):
                for dr in range(2):
                    for dh in range(2):
                        corners.append(x_ref[c, r + dr, start + dh : start + dh + chunk, :])
            eff, kept = eff_ref[r, rows, :], kept_ref[r, rows, :]
            for q in range(4):
                row = (4 * comp + q) * 12
                force = stiff_ref[row] * corners[0]
                for k in range(1, 12):
                    force = force + stiff_ref[row + k] * corners[k]
                stress_out_ref[q, r, rows, :] = kept * stress_ref[q, r, rows, :] + eff * force


def potential_kernel(recv_ref, shear_ref, relax_ref, out_ref, eff_ref, kept_ref):
    relax = relax_ref[...]
    share = 1.0 / (1.0 + 0.5 * relax)
    eff_ref[...] = shear_ref[...] * share
    kept_ref[...] = (1.0 - 0.5 * relax) * share
    blocks = [jnp.transpose(recv_ref[pl.ds(k, LANES, stride=MID_TILES), :]) for k in range(3)]
    lines = jnp.concatenate(blocks, 0)
    for part in range(2):
        for r in range(2):
            start = 96 * (2 * part + r)
            out_ref[:, r, tile_of(part)] = lines[start : start + 96]


def whole(shape):
    return pl.BlockSpec(shape, lambda *_: (0,) * len(shape))


smem = pl.BlockSpec(memory_space=pltpu.SMEM)


def far_memory(x):
    return pltpu.with_memory_space_constraint(x, pltpu.HBM)


def exchanged(lines):
    count = lines.shape[0]
    rows = lines.reshape(LANES, 1, count)
    return lax.all_to_all(rows, ALL, 0, 0, tiled=True).reshape(count, LANES)


def params(mib):
    return pltpu.CompilerParams(vmem_limit_bytes=mib * 2**20)


def body(load, previous, stress_old, shear_modulus, relaxation, density_jump, element_stiffness,
         degree_slots):
    tile_place = lax.axis_index(TILE)
    place = (lax.axis_index(CAP) * 8 + tile_place).astype(jnp.int32).reshape(1)
    parity = (tile_place % 2).astype(jnp.int32).reshape(1)
    stiff = element_stiffness.reshape(144)
    slots = jnp.pad(degree_slots.reshape(8, 96), ((0, 0), (0, 32)), constant_values=-1)
    (fh, fl), (th, tl), twiddle = transform_tables()
    ratio, scale, radius = radial_tables()

    one = pl.BlockSpec((1, 2, COLS, LANES), lambda c: (c, 0, 0, 0))
    four = pl.BlockSpec((4, 2, COLS, LANES), lambda c: (c, 0, 0, 0))
    field = whole((2, COLS, LANES))
    packed = pl.pallas_call(
        pack_kernel,
        grid=(3,),
        in_specs=[smem, smem, one, one, four, field, field],
        out_specs=whole((IN_TILES * LANES, LANES)),
        out_shape=pltpu.HBM((IN_TILES * LANES, LANES), f32),
        scratch_shapes=[pltpu.VMEM((3, COLS, LANES), f32), pltpu.VMEM((256, LANES), f32)],
        compiler_params=params(12),
    )(parity, *[far_memory(x) for x in (density_jump, load, previous, stress_old, shear_modulus, relaxation)])
    received = exchanged(packed)

    basis, sent = pl.pallas_call(
        functools.partial(section_kernel, radius=[float(x) for x in radius]),
        in_specs=[smem] + [pl.BlockSpec(memory_space=pltpu.VMEM)] * 9,
        out_specs=[pl.BlockSpec(memory_space=pl.ANY), pl.BlockSpec(memory_space=pltpu.VMEM)],
        out_shape=[
            pltpu.HBM((7, 96, HRING), f32),
            pltpu.HBM((MID_TILES * LANES, LANES), f32),
        ],
        scratch_shapes=[
            pltpu.VMEM((8, 96, HRING), f32),
            pltpu.SemaphoreType.DMA((7,)),
            pltpu.VMEM((4, 32, HRING), f32),
            pltpu.VMEM((2, 384, 256), bf16),
            pltpu.VMEM((384, HRING), bf16),
            pltpu.VMEM((384, HRING), bf16),
            pltpu.VMEM((96, HRING), f32),
            pltpu.VMEM((512, LANES), f32),
            pltpu.VMEM((NR, 8, 256), f32),
        ],
        compiler_params=params(20),
    )(stiff, received, slots, fh, fl, th, tl, twiddle, ratio, scale)
    shared = exchanged(sent)

    back = pl.pallas_call(
        solve_kernel,
        grid=(1,),
        in_specs=[
            smem,
            whole((MID_TILES * LANES, LANES)),
            pl.BlockSpec(memory_space=pl.ANY),
        ],
        out_specs=whole((OUT_TILES * LANES, LANES)),
        out_shape=pltpu.HBM((OUT_TILES * LANES, LANES), f32),
        scratch_shapes=[
            pltpu.VMEM((96, HRING), f32),
            pltpu.VMEM((7, 96, HRING), f32),
            pltpu.SemaphoreType.DMA((7,)),
        ],
        compiler_params=params(12),
    )(place, shared, far_memory(basis))
    returned = exchanged(back)

    potential, effective, kept = pl.pallas_call(
        potential_kernel,
        grid=(1,),
        in_specs=[whole((MID_TILES * LANES, LANES)), field, field],
        out_specs=[whole((96, 2, 256)), field, field],
        out_shape=[jax.ShapeDtypeStruct((96, 2, 256), f32)]
        + [pltpu.HBM((2, COLS, LANES), f32)] * 2,
        compiler_params=params(4),
    )(shared, far_memory(shear_modulus), far_memory(relaxation))

    displacement, stress_new = pl.pallas_call(
        finish_kernel,
        grid=(3,),
        in_specs=[smem, smem, whole((OUT_TILES * LANES, LANES)), four, field, field],
        out_specs=[whole((3, 2, COLS, LANES)), four],
        out_shape=[
            jax.ShapeDtypeStruct((3, 2, COLS, LANES), f32),
            jax.ShapeDtypeStruct((12, 2, COLS, LANES), f32),
        ],
        scratch_shapes=[
            pltpu.VMEM((3, 3, COLS + 8, LANES), f32),
        ],
        compiler_params=params(12),
    )(parity, stiff, returned, stress_old, far_memory(effective), far_memory(kept))
    return displacement, stress_new, potential


def solution(mesh):
    torus = Mesh(mesh.devices.reshape(4, 4, 4, 2), ("cap_0", "cap_1", "tile_0", "tile_1"))
    return jax.shard_map(
        body,
        mesh=torus,
        in_specs=(
            P(None, CAP, TILE, None),
            P(None, CAP, TILE, None),
            P(None, CAP, TILE, None),
            P(CAP, TILE, None),
            P(CAP, TILE, None),
            P(CAP),
            P(),
            P(),
        ),
        out_specs=(P(None, CAP, TILE, None), P(None, CAP, TILE, None), P(TILE, CAP, None)),
        check_vma=False,
    )
```

```python
import functools
import math

import jax
import jax.numpy as jnp
import ml_dtypes
import numpy as np
from jax import lax
from jax.experimental import pallas as pl
from jax.experimental.pallas import tpu as pltpu
from jax.sharding import Mesh
from jax.sharding import PartitionSpec as P

HRING = 1536
LDEG = 768
NR = 32
TILE = ("tile_0", "tile_1")
CAP = ("cap_0", "cap_1")
ALL = ("cap_0", "cap_1", "tile_0", "tile_1")
LANES = 128
COLS = 192
ROOT3H = math.sqrt(3.0) / 2.0
rotation_gain = 2.0
gravity_gain = 0.2

EFF_TILE = 21
TAIL_TILE = 24
IN_TILES = 26
MID_TILES = 4
OUT_TAIL = 12
OUT_TILES = 14

f32 = jnp.float32
bf16 = jnp.bfloat16


def split_table(table):
    high = table.astype(ml_dtypes.bfloat16)
    low = (table - high.astype(np.float64)).astype(ml_dtypes.bfloat16)
    return high, low


def transform_tables():
    q = np.arange(128)[None, :]
    b = np.arange(256)[:, None]
    angle = 2.0 * np.pi * ((q * b) % 256) / 256.0
    cosine, sine = np.cos(angle), np.sin(angle)
    table = np.concatenate(
        [np.concatenate([cosine, sine], 1), np.concatenate([sine, -cosine], 1)], 0
    )
    p = np.arange(8)[:, None]
    turn = 2.0 * np.pi * ((p * np.arange(256)[None, :]) % HRING) / HRING
    twiddle = np.stack([np.cos(turn), np.sin(turn)]).astype(np.float32)
    return split_table(table), split_table(np.ascontiguousarray(table.T)), twiddle


def radial_tables():
    radius = 1.0 - 0.45 * (np.arange(NR) + 0.5) / NR
    degree = 6.0 * np.arange(128)[None, :] + np.arange(8)[:, None]
    log_radius = np.log(radius)
    ratio = np.zeros((NR, 8, 128))
    for r in range(1, NR):
        ratio[r] = np.exp(-degree * (log_radius[r - 1] - log_radius[r]))
    scale = 1.0 / np.sqrt(2.0 * degree + 1.0)
    return ratio.astype(np.float32), scale.astype(np.float32), radius


def split(x):
    high = x.astype(bf16)
    return high, (x - high.astype(f32)).astype(bf16)


def mm(a, b):
    return jnp.dot(a, b, preferred_element_type=f32)


def lane_index(shape):
    return lax.broadcasted_iota(jnp.int32, shape, len(shape) - 1)


def row_index(shape):
    return lax.broadcasted_iota(jnp.int32, shape, 0)


def tile_of(k):
    return slice(k * LANES, (k + 1) * LANES)


def down_one(x):
    return jnp.where(row_index(x.shape) == 0, 0.0, pltpu.roll(x, 1, 0))


def up_one(x):
    n = x.shape[0]
    return jnp.where(row_index(x.shape) == n - 1, 0.0, pltpu.roll(x, n - 1, 0))


def pack_kernel(parity_ref, density_ref, load_ref, prev_ref, stress_ref, shear_ref, relax_ref,
                out_ref, acc_ref, tail_ref):
    comp = pl.program_id(0)
    parity = parity_ref[0]
    wide = pl.ds(pl.multiple_of(64 * parity, 64), 128)
    narrow = pl.ds(pl.multiple_of(128 * (1 - parity), 64), 64)

    def put(tile, block):
        out_ref[pl.ds(tile, LANES, stride=IN_TILES), :] = jnp.transpose(block)

    @pl.when(comp == 0)
    def _():
        acc_ref[:2] = shear_ref[...] / (1.0 + 0.5 * relax_ref[...])
        put(EFF_TILE, acc_ref[0, wide, :])
        put(EFF_TILE + 1, acc_ref[1, wide, :])
        put(EFF_TILE + 2, jnp.concatenate([acc_ref[0, narrow, :], acc_ref[1, narrow, :]], 0))
        tail_ref[192:256, :] = jnp.zeros((64, LANES), f32)
        for r in range(2):
            tail_ref[201 + r : 202 + r, :] = jnp.full((1, LANES), density_ref[r], f32)

    base = comp * 7
    put(base, prev_ref[0, 0, wide, :])
    put(base + 1, prev_ref[0, 1, wide, :])
    put(base + 2, jnp.concatenate([prev_ref[0, 0, narrow, :], prev_ref[0, 1, narrow, :]], 0))

    relax = relax_ref[...]
    carried = relax / (1.0 + 0.5 * relax)
    part = [[carried[r] * stress_ref[q, r] for r in range(2)] for q in range(4)]
    near = [part[0][0], part[0][1] + part[2][0], part[2][1]]
    far = [part[1][0], part[1][1] + part[3][0], part[3][1]]
    for r in range(3):
        total = near[r] + down_one(far[r])
        if r < 2:
            total = total + load_ref[0, r]
        acc_ref[r] = total
        tail_ref[pl.ds(192 + 3 * comp + r, 1), :] = far[r][COLS - 1 : COLS, :]
    for r in range(3):
        put(base + 3 + r, acc_ref[r, wide, :])
    put(base + 6, jnp.concatenate([acc_ref[0, narrow, :], acc_ref[1, narrow, :]], 0))
    tail_ref[pl.ds(pl.multiple_of(64 * comp, 64), 64), :] = acc_ref[2, narrow, :]

    @pl.when(comp == 2)
    def _():
        put(TAIL_TILE, tail_ref[:128, :])
        put(TAIL_TILE + 1, tail_ref[128:, :])


def section_kernel(stiff_ref, recv_ref, slots_ref, fh_ref, fl_ref, th_ref, tl_ref, twiddle_ref,
                   ratio_ref, scale_ref, kept_ref, send_ref, basis_ref, sems,
                   eff_ref, matrix_ref, xh_ref, xl_ref, image_ref, coef_ref, pot_ref,
                   *, radius):
    lane = lane_index((16, LANES))

    def leaving(slot):
        return pltpu.make_async_copy(basis_ref.at[slot + 1], kept_ref.at[slot], sems.at[slot])

    def rows_of(t, tile):
        return recv_ref[pl.ds(IN_TILES * t + tile, 16, stride=8 * IN_TILES), :]

    def unrolled(wide_tile, narrow_tile, half):
        for u in range(4):
            even, odd = rows_of(2 * u, narrow_tile), rows_of(2 * u + 1, narrow_tile)
            if half == 0:
                middle = jnp.where(lane < 64, even, pltpu.roll(odd, 64, 1))
            else:
                middle = jnp.where(lane < 64, pltpu.roll(even, 64, 1), odd)
            yield 3 * u, rows_of(2 * u, wide_tile)
            yield 3 * u + 1, middle
            yield 3 * u + 2, rows_of(2 * u + 1, wide_tile)

    tail = TAIL_TILE
    for c in range(3):
        for r in range(2):
            rows = slice(32 * c + 16 * r, 32 * c + 16 * r + 16)
            for k, block in unrolled(7 * c + r, 7 * c + 2, r):
                basis_ref[1, rows, tile_of(k)] = block
            for k, block in unrolled(7 * c + 3 + r, 7 * c + 6, r):
                basis_ref[0, rows, tile_of(k)] = block
        rows = slice(32 * c, 32 * c + 16)
        for k, block in unrolled(7 * c + 5, tail + c // 2, c % 2):
            basis_ref[0, rows, tile_of(k)] += down_one(block)
    leaving(0).start()
    for t in range(8):
        following = (t + 1) % 8
        k, target = 3 * (following // 2) + following % 2, 64 * (following % 2)
        block = rows_of(t, tail + 1)
        for c in range(3):
            for r in range(3):
                shift = (target - 64 - 3 * c - r) % LANES
                value = jnp.where(lane == target, pltpu.roll(block, shift, 1), 0.0)
                if r == 2:
                    value = down_one(value)
                start = 32 * c + 16 * (r % 2)
                basis_ref[0, start : start + 16, tile_of(k)] += value
    for r in range(2):
        for k, block in unrolled(EFF_TILE + r, EFF_TILE + 2, r):
            eff_ref[0, 16 * r : 16 * r + 16, tile_of(k)] = block
    eff_ref[1, 16:32, :] = eff_ref[0, 0:16, :]
    eff_ref[1, 0:16, :] = down_one(eff_ref[0, 16:32, :])

    density = jnp.concatenate(
        [jnp.sum(jnp.where(lane == 73 + r, rows_of(0, tail + 1), 0.0), 1, keepdims=True)
         for r in range(2)], 0
    )

    weight = density * math.sqrt(2.0 / HRING)
    w = [basis_ref[1, 0:32, 256 * a : 256 * a + 256] * weight for a in range(6)]
    s1, s2, d1, d2 = w[1] + w[5], w[2] + w[4], w[1] - w[5], w[2] - w[4]
    plus, minus = w[0] + w[3], w[0] - w[3]
    half = 0.5 * (s1 + s2)
    diff = 0.5 * (s1 - s2)
    real = [plus + 2.0 * half, minus + diff, plus - half, minus - 2.0 * diff]
    real += [real[2], real[1]]
    i1, i2 = -ROOT3H * (d1 + d2), -ROOT3H * (d1 - d2)
    imag = [None, i1, i2, None, -i2, -i1]
    for p in range(6):
        cosine, sine = twiddle_ref[0, p : p + 1, :], twiddle_ref[1, p : p + 1, :]
        rows = slice(32 * p, 32 * p + 32)
        re, im = real[p] * cosine, -real[p] * sine
        if imag[p] is not None:
            re, im = re + imag[p] * sine, im + imag[p] * cosine
        for k, x in ((0, re), (256, im)):
            high, low = split(x)
            xh_ref[rows, k : k + 256] = high
            xl_ref[rows, k : k + 256] = low
    high, low = xh_ref[0:192, 0:512], xl_ref[0:192, 0:512]
    coefs = mm(high, fh_ref[...]) + mm(low, fh_ref[...]) + mm(high, fl_ref[...])
    for k in range(2):
        coef_ref[256 * k : 256 * k + 192, :] = coefs[:, tile_of(k)]
        coef_ref[256 * k + 192 : 256 * k + 256, :] = jnp.zeros((64, LANES), f32)

    def place(r, k):
        return pl.ds(256 * k + 16 * (r % 2) + r // 2, 8, stride=32)

    zero = jnp.zeros((8, LANES), f32)
    for k in range(2):
        lanes = tile_of(k)
        rows = [coef_ref[place(r, k), :] for r in range(NR)]
        forward, moment = zero, zero
        for r in range(NR):
            forward = rows[r] + ratio_ref[r] * forward
            moment = moment + (radius[r] ** 4 / NR) * rows[r]
            pot_ref[r, :, lanes] = forward
        chosen = (lane_index((8, LANES)) == 0) & (row_index((8, LANES)) == 2)
        moment = jnp.where(chosen, rotation_gain * moment, 0.0)
        back = zero
        for r in reversed(range(NR)):
            if r + 1 < NR:
                back = ratio_ref[r + 1] * (rows[r + 1] + back)
            pot_ref[r, :, lanes] = (
                (pot_ref[r, :, lanes] + back) * scale_ref[...] + radius[r] ** 2 * moment
            )
    for k in range(2):
        for r in range(NR):
            coef_ref[place(r, k), :] = pot_ref[r, :, tile_of(k)]

    for k in range(2):
        for p in range(6):
            x = coef_ref[256 * k + 32 * p : 256 * k + 32 * p + 32, :]
            high, low = split(x)
            rest = (x - high.astype(f32) - low.astype(f32)).astype(bf16)
            for n, piece in enumerate((high, low, rest)):
                xl_ref[64 * n + 32 * k : 64 * n + 32 * k + 32, tile_of(p)] = piece
    degrees = slots_ref[...]
    for t in range(8):
        d = degrees[t : t + 1, :]
        where_from = (d % 6) * LANES + d // 6
        pick = jnp.where(row_index((LDEG, LANES)) == where_from, 1.0, 0.0).astype(bf16)
        chosen = mm(xl_ref[0:192, 0:LDEG], pick)
        chosen = chosen[0:64] + chosen[64:128] + chosen[128:192]
        c0, c1, c2, c3 = [chosen[16 * k : 16 * k + 16] for k in range(4)]
        joined = [
            jnp.where(lane < 96, c0, pltpu.roll(c1, 96, 1)),
            jnp.where(lane < 64, pltpu.roll(c1, 96, 1), pltpu.roll(c2, 64, 1)),
            jnp.where(lane < 32, pltpu.roll(c2, 64, 1), pltpu.roll(c3, 32, 1)),
        ]
        for k, block in enumerate(joined):
            send_ref[pl.ds(MID_TILES * t + k, 16, stride=8 * MID_TILES), :] = block

    high, low = split(jnp.concatenate([coef_ref[0:192, :], coef_ref[256:448, :]], 1))
    field = mm(high, th_ref[...]) + mm(low, th_ref[...]) + mm(high, tl_ref[...])
    re, im = [], []
    for p in range(6):
        cosine, sine = twiddle_ref[0, p : p + 1, :], twiddle_ref[1, p : p + 1, :]
        x, y = field[32 * p : 32 * p + 32, 0:256], field[32 * p : 32 * p + 32, 256:512]
        re.append(x * cosine - y * sine)
        im.append(x * sine + y * cosine)
    a1, a2, e1, e2 = re[1] + re[5], re[2] + re[4], im[1] - im[5], im[2] - im[4]
    plus, minus = re[0] + re[3], re[0] - re[3]
    half, diff = 0.5 * (a1 + a2), 0.5 * (a1 - a2)
    o1, o2 = ROOT3H * (e1 + e2), ROOT3H * (e1 - e2)
    parts = [plus + 2.0 * half, minus + diff - o1, plus - half - o2, minus - 2.0 * diff,
             plus - half + o2, minus + diff + o1]
    for a in range(6):
        basis_ref[0, 0:32, 256 * a : 256 * a + 256] += gravity_gain * density * parts[a]

    idx = row_index((32, LANES))
    lane32 = lane_index((32, LANES))
    after = jnp.where(idx < 16, idx + 16, jnp.where(idx == 31, -1000, idx - 15))
    before = jnp.where(idx >= 16, idx - 16, jnp.where(idx == 0, -1000, idx + 15))
    masks = {}
    for c in range(3):
        for name, index in ((0, idx), (1, after), (-1, before)):
            masks[c, name] = jnp.where(lane32 == index + 32 * c, 1.0, 0.0)
    for q in range(4):
        for c in range(3):
            row, start = 4 * c + q, 96 * q + 32 * c
            for dh in range(2):
                block = jnp.zeros((32, LANES), f32)
                for c2 in range(3):
                    for dr in range(2):
                        value = stiff_ref[12 * row + 4 * c2 + 2 * dr + dh]
                        block = block + value * masks[c2, dr - q // 2]
                high, low = split(block)
                matrix_ref[start : start + 32, tile_of(dh)] = high
                matrix_ref[384 + start : 416 + start, tile_of(dh)] = low

    for k in range(2):
        pad = jnp.zeros((32, HRING), bf16)
        xh_ref[128 * k + 96 : 128 * k + 128, :] = pad
        xl_ref[128 * k + 96 : 128 * k + 128, :] = pad

    lane_row = lane_index((1, LANES))

    def total(x):
        return jnp.sum(jnp.sum(x, 0, keepdims=True), 1, keepdims=True)

    def spread(v):
        for k, x in ((0, v), (128, pltpu.roll(v, HRING - 1, 1))):
            high, low = split(x)
            xh_ref[k : k + 96, :] = high
            xl_ref[k : k + 96, :] = low

    first_lane = lane_index((96, 256)) == 0

    def products(n, image, j):
        cols = slice(256 * n, 256 * n + 256)
        v, before = basis_ref[j + 1, :, cols], basis_ref[j, :, cols]
        return image * v, image * image, image * before

    def apply(j):
        carry, sums = None, None
        for n in range(6):
            cols = slice(256 * n, 256 * n + 256)
            first = mm(matrix_ref[...], xh_ref[:, cols])
            second = mm(matrix_ref[0:384, :], xl_ref[:, cols])
            force = (first[0:384] + first[384:768] + second).reshape(4, 3, 32, 256)
            here, above = eff_ref[0, :, cols][None], eff_ref[1, :, cols][None]
            image = (force[0] * here + force[2] * above).reshape(96, 256)
            passed = pltpu.roll((force[1] * here + force[3] * above).reshape(96, 256), 1, 1)
            if n == 0:
                image_ref[:, cols] = image + jnp.where(first_lane, 0.0, passed)
            else:
                image = image + jnp.where(first_lane, carry, passed)
                image_ref[:, cols] = image
                terms = products(n, image, j)
                sums = terms if sums is None else [x + y for x, y in zip(sums, terms)]
            carry = passed
        image = image_ref[:, 0:256] + jnp.where(first_lane, carry, 0.0)
        image_ref[:, 0:256] = image
        return [total(x + y) for x, y in zip(sums, products(0, image, j))]

    def inverted(x):
        return jnp.where(x > 0.0, 1.0 / x, 0.0)

    def root(x):
        return jnp.where(x > 0.0, x * lax.rsqrt(x), 0.0)

    spread(basis_ref[1])
    load_norm = total(basis_ref[0] * basis_ref[0])
    _, image_norm, cross = apply(0)
    rough = jnp.maximum(image_norm - 2.0 * cross + load_norm, 1e-6 * (image_norm + load_norm))
    scale = jnp.where(rough > 0.0, lax.rsqrt(rough), 0.0)

    def step(j, state):
        moments, a, b, scale, norm_before = state
        v = scale * (image_ref[...] - a * basis_ref[j] - b * basis_ref[j - 1])
        basis_ref[j + 1] = v
        leaving(j).start()
        norm = total(v * v)
        spread(v)
        inner, image_norm, cross = apply(j)
        inverse = inverted(norm)
        a = inner * inverse
        b = jnp.where(j == 1, 0.0, cross * inverted(norm_before))
        beside = root(norm) * inverted(jnp.abs(scale) * root(norm_before))
        moments = (
            moments
            + jnp.where(lane_row == j - 1, a, 0.0)
            + jnp.where(lane_row == jnp.where(j == 1, 16, 6 + j), beside, 0.0)
            + jnp.where(lane_row == 23 + j, root(inverse), 0.0)
        )
        rough = jnp.maximum(image_norm - a * inner - b * cross, 1e-6 * image_norm)
        scale = jnp.where(rough > 0.0, lax.rsqrt(rough), 0.0)
        return moments, a, b, scale, norm

    one = jnp.ones((1, 1), f32)
    moments = lax.fori_loop(
        1, 7, step, (jnp.zeros((1, LANES), f32), 0.0 * one, one, -scale, one)
    )[0]
    send_ref[pl.ds(3, LANES, stride=MID_TILES), :] = jnp.broadcast_to(moments, (LANES, LANES))
    for slot in range(7):
        leaving(slot).wait()


def solve_kernel(place_ref, moments_ref, kept_ref, out_ref, x_ref, basis_ref, sems):
    def arriving(slot):
        return pltpu.make_async_copy(kept_ref.at[slot], basis_ref.at[slot], sems.at[slot])

    for slot in range(7):
        arriving(slot).start()
    table = jnp.transpose(moments_ref[pl.ds(3, LANES, stride=MID_TILES), :])
    diagonal, beside, start = table[0:8], table[8:16], table[16:17]
    first = row_index((8, LANES)) == 0
    residual = jnp.where(first, start, 0.0)

    def total(x):
        return jnp.sum(jnp.sum(x, 0, keepdims=True), 1, keepdims=True)

    def applied(v):
        return (
            diagonal * v
            + beside * pltpu.roll(v, 7, 0)
            + pltpu.roll(beside * v, 1, 0)
        )

    image = applied(residual)
    norm, product = total(residual * residual), total(residual * image)
    size = norm / product
    direction, along, y = residual, image, size * residual
    for i in range(5):
        residual = residual - size * along
        image = applied(residual)
        new, product = total(residual * residual), total(residual * image)
        growth = new / norm
        size = new / (product - growth * new / size)
        direction, along = residual + growth * direction, image + growth * along
        y, norm = y + size * direction, new
    mine = lane_index((8, LANES)) == place_ref[0]
    own = jnp.sum(jnp.where(mine, y * table[24:32], 0.0), 1, keepdims=True)
    for group in ((0, 1, 2), (3, 4), (5, 6)):
        for slot in group:
            arriving(slot).wait()
        x = basis_ref[0] if group[0] == 0 else x_ref[...]
        for slot in group:
            if slot:
                x = x + own[slot - 1 : slot, :] * basis_ref[slot]
        x_ref[...] = x

    lane = lane_index((16, LANES))

    def node_rows(c, r, k):
        block = x_ref[32 * c + 16 * (r % 2) : 32 * c + 16 * (r % 2) + 16, tile_of(k)]
        return up_one(block) if r == 2 else block

    def at(t, tile):
        return pl.ds(OUT_TILES * t + tile, 16, stride=8 * OUT_TILES)

    for u in range(4):
        even, odd = 2 * u, 2 * u + 1
        for c in range(3):
            for r in range(3):
                out_ref[at(even, 4 * c + r), :] = node_rows(c, r, 3 * u)
                out_ref[at(odd, 4 * c + r), :] = node_rows(c, r, 3 * u + 2)
            low, high = node_rows(c, 0, 3 * u + 1), node_rows(c, 1, 3 * u + 1)
            out_ref[at(even, 4 * c + 3), :] = jnp.where(lane < 64, low, pltpu.roll(high, 64, 1))
            out_ref[at(odd, 4 * c + 3), :] = jnp.where(lane < 64, pltpu.roll(low, 64, 1), high)
        extra = [node_rows(c, 2, 3 * u + 1) for c in range(3)]
        out_ref[at(even, OUT_TAIL), :] = jnp.where(
            lane < 64, extra[0], pltpu.roll(extra[1], 64, 1)
        )
        out_ref[at(odd, OUT_TAIL), :] = jnp.where(
            lane < 64, pltpu.roll(extra[0], 64, 1), extra[1]
        )
        for parity, rows in ((0, even), (1, odd)):
            block = extra[2] if parity == 0 else pltpu.roll(extra[2], 64, 1)
            following = (2 * u + parity + 1) % 8
            k, source = 3 * (following // 2) + following % 2, 64 * (following % 2)
            for c in range(3):
                for r in range(3):
                    target = 64 + 3 * c + r
                    value = pltpu.roll(node_rows(c, r, k), (target - source) % LANES, 1)
                    block = jnp.where(lane == target, value, block)
            out_ref[at(rows, OUT_TAIL + 1), :] = block


def finish_kernel(parity_ref, stiff_ref, recv_ref, stress_ref, shear_far_ref, relax_far_ref,
                  x_out_ref, stress_out_ref, x_ref, new_ref, matrix_ref, shear_ref, relax_ref,
                  first_ref, x_sems, sems):
    shear_arriving = pltpu.make_async_copy(shear_far_ref, shear_ref, sems.at[3])
    relax_arriving = pltpu.make_async_copy(relax_far_ref, relax_ref, sems.at[4])
    shear_arriving.start()
    relax_arriving.start()
    parity = parity_ref[0]
    wide = pl.ds(pl.multiple_of(64 * parity, 64), 128)
    narrow = pl.ds(pl.multiple_of(128 * (1 - parity), 64), 64)

    def block(k):
        return jnp.transpose(recv_ref[pl.ds(k, LANES, stride=OUT_TILES), :])

    def x_leaving(c):
        return pltpu.make_async_copy(x_ref.at[c, 0:2, 0:COLS], x_out_ref.at[c], x_sems.at[c])

    def leaving(part):
        rows = pl.ds(64 * part, 64)
        return pltpu.make_async_copy(
            new_ref.at[:, :, rows], stress_out_ref.at[:, :, rows], sems.at[part]
        )

    for c in range(3):
        for r in range(3):
            x_ref[c, r, wide, :] = block(4 * c + r)
        rest = block(4 * c + 3)
        x_ref[c, 0, narrow, :] = rest[0:64]
        x_ref[c, 1, narrow, :] = rest[64:128]
        x_leaving(c).start()
    rest = block(OUT_TAIL)
    x_ref[0, 2, narrow, :] = rest[0:64]
    x_ref[1, 2, narrow, :] = rest[64:128]
    rest = block(OUT_TAIL + 1)
    x_ref[2, 2, narrow, :] = rest[0:64]
    for c in range(3):
        for r in range(3):
            x_ref[c, r, COLS : COLS + 1, :] = rest[64 + 3 * c + r : 65 + 3 * c + r]

    lane = lane_index((16, 192))
    same = (lane % 16) == row_index((16, 192))
    for a in range(12):
        line = jnp.zeros((16, 192), f32)
        for b in range(12):
            line = jnp.where(lane // 16 == b, stiff_ref[12 * a + b], line)
        high, low = split(jnp.where(same, line, 0.0))
        for k, piece in enumerate((high, high, low)):
            matrix_ref[16 * a : 16 * a + 16, 256 * k : 256 * k + 192] = piece
            matrix_ref[16 * a : 16 * a + 16, 256 * k + 192 : 256 * k + 256] = jnp.zeros(
                (16, 64), bf16
            )

    pad = jnp.zeros((64, 2 * LANES), bf16)

    def forces(n):
        corners = []
        for c in range(3):
            for dr in range(2):
                for dh in range(2):
                    span = slice(16 * n + dh, 16 * n + dh + 16)
                    corners.append(
                        jnp.concatenate([x_ref[c, dr, span, :], x_ref[c, 1 + dr, span, :]], 1)
                    )
        high, low = split(jnp.concatenate(corners, 0))
        return mm(matrix_ref[...], jnp.concatenate([high, pad, low, pad, high, pad], 0))

    def store(n, force):
        rows = slice(16 * n, 16 * n + 16)
        for r in range(2):
            relax = relax_ref[r, rows, :]
            share = 1.0 / (1.0 + 0.5 * relax)
            eff, kept = shear_ref[r, rows, :] * share, (1.0 - 0.5 * relax) * share
            for a in range(12):
                new_ref[a, r, rows, :] = (
                    kept * stress_ref[a, r, rows, :]
                    + eff * force[16 * a : 16 * a + 16, tile_of(r)]
                )

    for n in range(4):
        first_ref[n] = forces(n)
    shear_arriving.wait()
    relax_arriving.wait()
    for n in range(4):
        store(n, first_ref[n])
    leaving(0).start()
    for n in range(4, COLS // 16):
        store(n, forces(n))
        if n % 4 == 3:
            leaving(n // 4).start()
    for c in range(3):
        x_leaving(c).wait()
    for part in range(3):
        leaving(part).wait()


def potential_kernel(recv_ref, out_ref):
    blocks = [jnp.transpose(recv_ref[pl.ds(k, LANES, stride=MID_TILES), :]) for k in range(3)]
    lines = jnp.concatenate(blocks, 0)
    for part in range(2):
        for r in range(2):
            start = 96 * (2 * part + r)
            out_ref[:, r, tile_of(part)] = lines[start : start + 96]


def whole(shape):
    return pl.BlockSpec(shape, lambda *_: (0,) * len(shape))


smem = pl.BlockSpec(memory_space=pltpu.SMEM)


def far_memory(x):
    return pltpu.with_memory_space_constraint(x, pltpu.HBM)


def exchanged(lines):
    count = lines.shape[0]
    rows = lines.reshape(LANES, 1, count)
    return lax.all_to_all(rows, ALL, 0, 0, tiled=True).reshape(count, LANES)


def params(mib):
    return pltpu.CompilerParams(vmem_limit_bytes=mib * 2**20)


def body(load, previous, stress_old, shear_modulus, relaxation, density_jump, element_stiffness,
         degree_slots):
    tile_place = lax.axis_index(TILE)
    place = (lax.axis_index(CAP) * 8 + tile_place).astype(jnp.int32).reshape(1)
    parity = (tile_place % 2).astype(jnp.int32).reshape(1)
    stiff = element_stiffness.reshape(144)
    slots = jnp.pad(degree_slots.reshape(8, 96), ((0, 0), (0, 32)), constant_values=-1)
    (fh, fl), (th, tl), twiddle = transform_tables()
    ratio, scale, radius = radial_tables()

    one = pl.BlockSpec((1, 2, COLS, LANES), lambda c: (c, 0, 0, 0))
    four = pl.BlockSpec((4, 2, COLS, LANES), lambda c: (c, 0, 0, 0))
    field = whole((2, COLS, LANES))
    packed = pl.pallas_call(
        pack_kernel,
        grid=(3,),
        in_specs=[smem, smem, one, one, four, field, field],
        out_specs=whole((IN_TILES * LANES, LANES)),
        out_shape=pltpu.HBM((IN_TILES * LANES, LANES), f32),
        scratch_shapes=[pltpu.VMEM((3, COLS, LANES), f32), pltpu.VMEM((256, LANES), f32)],
        compiler_params=params(12),
    )(parity, *[far_memory(x) for x in (density_jump, load, previous, stress_old, shear_modulus, relaxation)])
    received = exchanged(packed)

    basis, sent = pl.pallas_call(
        functools.partial(section_kernel, radius=[float(x) for x in radius]),
        in_specs=[smem] + [pl.BlockSpec(memory_space=pltpu.VMEM)] * 9,
        out_specs=[pl.BlockSpec(memory_space=pl.ANY), pl.BlockSpec(memory_space=pltpu.VMEM)],
        out_shape=[
            pltpu.HBM((7, 96, HRING), f32),
            pltpu.HBM((MID_TILES * LANES, LANES), f32),
        ],
        scratch_shapes=[
            pltpu.VMEM((8, 96, HRING), f32),
            pltpu.SemaphoreType.DMA((7,)),
            pltpu.VMEM((2, 32, HRING), f32),
            pltpu.VMEM((768, 256), bf16),
            pltpu.VMEM((256, HRING), bf16),
            pltpu.VMEM((256, HRING), bf16),
            pltpu.VMEM((96, HRING), f32),
            pltpu.VMEM((512, LANES), f32),
            pltpu.VMEM((NR, 8, 256), f32),
        ],
        compiler_params=params(20),
    )(stiff, received, slots, fh, fl, th, tl, twiddle, ratio, scale)
    shared = exchanged(sent)

    back = pl.pallas_call(
        solve_kernel,
        grid=(1,),
        in_specs=[
            smem,
            whole((MID_TILES * LANES, LANES)),
            pl.BlockSpec(memory_space=pl.ANY),
        ],
        out_specs=whole((OUT_TILES * LANES, LANES)),
        out_shape=pltpu.HBM((OUT_TILES * LANES, LANES), f32),
        scratch_shapes=[
            pltpu.VMEM((96, HRING), f32),
            pltpu.VMEM((7, 96, HRING), f32),
            pltpu.SemaphoreType.DMA((7,)),
        ],
        compiler_params=params(12),
    )(place, shared, far_memory(basis))
    returned = exchanged(back)

    potential = pl.pallas_call(
        potential_kernel,
        grid=(1,),
        in_specs=[whole((MID_TILES * LANES, LANES))],
        out_specs=whole((96, 2, 256)),
        out_shape=jax.ShapeDtypeStruct((96, 2, 256), f32),
        compiler_params=params(4),
    )(shared)

    displacement, stress_new = pl.pallas_call(
        finish_kernel,
        in_specs=[smem, smem]
        + [pl.BlockSpec(memory_space=pltpu.VMEM)] * 2
        + [pl.BlockSpec(memory_space=pl.ANY)] * 2,
        out_specs=[pl.BlockSpec(memory_space=pl.ANY)] * 2,
        out_shape=[
            jax.ShapeDtypeStruct((3, 2, COLS, LANES), f32),
            jax.ShapeDtypeStruct((12, 2, COLS, LANES), f32),
        ],
        scratch_shapes=[
            pltpu.VMEM((3, 3, COLS + 8, LANES), f32),
            pltpu.VMEM((12, 2, COLS, LANES), f32),
            pltpu.VMEM((192, 768), bf16),
            pltpu.VMEM((2, COLS, LANES), f32),
            pltpu.VMEM((2, COLS, LANES), f32),
            pltpu.VMEM((4, COLS, 2 * LANES), f32),
            pltpu.SemaphoreType.DMA((3,)),
            pltpu.SemaphoreType.DMA((5,)),
        ],
        compiler_params=params(12),
    )(parity, stiff, returned, stress_old, far_memory(shear_modulus), far_memory(relaxation))
    return displacement, stress_new, potential


def solution(mesh):
    torus = Mesh(mesh.devices.reshape(4, 4, 4, 2), ("cap_0", "cap_1", "tile_0", "tile_1"))
    return jax.shard_map(
        body,
        mesh=torus,
        in_specs=(
            P(None, CAP, TILE, None),
            P(None, CAP, TILE, None),
            P(None, CAP, TILE, None),
            P(CAP, TILE, None),
            P(CAP, TILE, None),
            P(CAP),
            P(),
            P(),
        ),
        out_specs=(P(None, CAP, TILE, None), P(None, CAP, TILE, None), P(TILE, CAP, None)),
        check_vma=False,
    )
```

```python
import functools
import math

import jax
import jax.numpy as jnp
import ml_dtypes
import numpy as np
from jax import lax
from jax.experimental import pallas as pl
from jax.experimental.pallas import tpu as pltpu
from jax.sharding import Mesh
from jax.sharding import PartitionSpec as P

HRING = 1536
LDEG = 768
NR = 32
TILE = ("tile_0", "tile_1")
CAP = ("cap_0", "cap_1")
ALL = ("cap_0", "cap_1", "tile_0", "tile_1")
LANES = 128
COLS = 192
ROOT3H = math.sqrt(3.0) / 2.0
rotation_gain = 2.0
gravity_gain = 0.2

EFF_TILE = 21
TAIL_TILE = 24
IN_TILES = 26
MID_TILES = 4
OUT_TAIL = 12
OUT_TILES = 14

f32 = jnp.float32
bf16 = jnp.bfloat16


def split_table(table):
    high = table.astype(ml_dtypes.bfloat16)
    low = (table - high.astype(np.float64)).astype(ml_dtypes.bfloat16)
    return high, low


def transform_tables():
    q = np.arange(128)[None, :]
    b = np.arange(256)[:, None]
    angle = 2.0 * np.pi * ((q * b) % 256) / 256.0
    cosine, sine = np.cos(angle), np.sin(angle)
    table = np.concatenate(
        [np.concatenate([cosine, sine], 1), np.concatenate([sine, -cosine], 1)], 0
    )
    p = np.arange(8)[:, None]
    turn = 2.0 * np.pi * ((p * np.arange(256)[None, :]) % HRING) / HRING
    twiddle = np.stack([np.cos(turn), np.sin(turn)]).astype(np.float32)
    return split_table(table), split_table(np.ascontiguousarray(table.T)), twiddle


def radial_tables():
    radius = 1.0 - 0.45 * (np.arange(NR) + 0.5) / NR
    degree = 6.0 * np.arange(128)[None, :] + np.arange(8)[:, None]
    log_radius = np.log(radius)
    ratio = np.zeros((NR, 8, 128))
    for r in range(1, NR):
        ratio[r] = np.exp(-degree * (log_radius[r - 1] - log_radius[r]))
    scale = 1.0 / np.sqrt(2.0 * degree + 1.0)
    return ratio.astype(np.float32), scale.astype(np.float32), radius


def split(x):
    high = x.astype(bf16)
    return high, (x - high.astype(f32)).astype(bf16)


def mm(a, b):
    return jnp.dot(a, b, preferred_element_type=f32)


def lane_index(shape):
    return lax.broadcasted_iota(jnp.int32, shape, len(shape) - 1)


def row_index(shape):
    return lax.broadcasted_iota(jnp.int32, shape, 0)


def tile_of(k):
    return slice(k * LANES, (k + 1) * LANES)


def down_one(x):
    return jnp.where(row_index(x.shape) == 0, 0.0, pltpu.roll(x, 1, 0))


def up_one(x):
    n = x.shape[0]
    return jnp.where(row_index(x.shape) == n - 1, 0.0, pltpu.roll(x, n - 1, 0))


def pack_kernel(parity_ref, density_ref, load_ref, prev_ref, stress_ref, shear_ref, relax_ref,
                out_ref, acc_ref, tail_ref):
    comp = pl.program_id(0)
    parity = parity_ref[0]
    wide = pl.ds(pl.multiple_of(64 * parity, 64), 128)
    narrow = pl.ds(pl.multiple_of(128 * (1 - parity), 64), 64)

    def put(tile, block):
        out_ref[pl.ds(tile, LANES, stride=IN_TILES), :] = jnp.transpose(block)

    @pl.when(comp == 0)
    def _():
        acc_ref[:2] = shear_ref[...] / (1.0 + 0.5 * relax_ref[...])
        put(EFF_TILE, acc_ref[0, wide, :])
        put(EFF_TILE + 1, acc_ref[1, wide, :])
        put(EFF_TILE + 2, jnp.concatenate([acc_ref[0, narrow, :], acc_ref[1, narrow, :]], 0))
        tail_ref[192:256, :] = jnp.zeros((64, LANES), f32)
        for r in range(2):
            tail_ref[201 + r : 202 + r, :] = jnp.full((1, LANES), density_ref[r], f32)

    base = comp * 7
    put(base, prev_ref[0, 0, wide, :])
    put(base + 1, prev_ref[0, 1, wide, :])
    put(base + 2, jnp.concatenate([prev_ref[0, 0, narrow, :], prev_ref[0, 1, narrow, :]], 0))

    relax = relax_ref[...]
    carried = relax / (1.0 + 0.5 * relax)
    part = [[carried[r] * stress_ref[q, r] for r in range(2)] for q in range(4)]
    near = [part[0][0], part[0][1] + part[2][0], part[2][1]]
    far = [part[1][0], part[1][1] + part[3][0], part[3][1]]
    for r in range(3):
        total = near[r] + down_one(far[r])
        if r < 2:
            total = total + load_ref[0, r]
        acc_ref[r] = total
        tail_ref[pl.ds(192 + 3 * comp + r, 1), :] = far[r][COLS - 1 : COLS, :]
    for r in range(3):
        put(base + 3 + r, acc_ref[r, wide, :])
    put(base + 6, jnp.concatenate([acc_ref[0, narrow, :], acc_ref[1, narrow, :]], 0))
    tail_ref[pl.ds(pl.multiple_of(64 * comp, 64), 64), :] = acc_ref[2, narrow, :]

    @pl.when(comp == 2)
    def _():
        put(TAIL_TILE, tail_ref[:128, :])
        put(TAIL_TILE + 1, tail_ref[128:, :])


def section_kernel(stiff_ref, recv_ref, slots_ref, fh_ref, fl_ref, th_ref, tl_ref, twiddle_ref,
                   ratio_ref, scale_ref, kept_ref, send_ref, basis_ref, sems,
                   eff_ref, matrix_ref, xh_ref, xl_ref, xs_ref, halo_ref, image_ref, coef_ref, pot_ref,
                   *, radius):
    lane = lane_index((16, LANES))

    def leaving(slot):
        return pltpu.make_async_copy(basis_ref.at[slot + 1], kept_ref.at[slot], sems.at[slot])

    def rows_of(t, tile):
        return recv_ref[pl.ds(IN_TILES * t + tile, 16, stride=8 * IN_TILES), :]

    def unrolled(wide_tile, narrow_tile, half):
        for u in range(4):
            even, odd = rows_of(2 * u, narrow_tile), rows_of(2 * u + 1, narrow_tile)
            if half == 0:
                middle = jnp.where(lane < 64, even, pltpu.roll(odd, 64, 1))
            else:
                middle = jnp.where(lane < 64, pltpu.roll(even, 64, 1), odd)
            yield 3 * u, rows_of(2 * u, wide_tile)
            yield 3 * u + 1, middle
            yield 3 * u + 2, rows_of(2 * u + 1, wide_tile)

    tail = TAIL_TILE

    def halves(c, r):
        for h in range(2):
            yield slice(8 * h, 8 * h + 8), slice(32 * c + 16 * h + 8 * r, 32 * c + 16 * h + 8 * r + 8)

    for c in range(3):
        for r in range(2):
            for k, block in unrolled(7 * c + r, 7 * c + 2, r):
                for part, rows in halves(c, r):
                    basis_ref[1, rows, tile_of(k)] = block[part]
            for k, block in unrolled(7 * c + 3 + r, 7 * c + 6, r):
                for part, rows in halves(c, r):
                    basis_ref[0, rows, tile_of(k)] = block[part]
        for k, block in unrolled(7 * c + 5, tail + c // 2, c % 2):
            block = down_one(block)
            for part, rows in halves(c, 0):
                basis_ref[0, rows, tile_of(k)] += block[part]
    leaving(0).start()
    for t in range(8):
        following = (t + 1) % 8
        k, target = 3 * (following // 2) + following % 2, 64 * (following % 2)
        block = rows_of(t, tail + 1)
        for c in range(3):
            for r in range(3):
                shift = (target - 64 - 3 * c - r) % LANES
                value = jnp.where(lane == target, pltpu.roll(block, shift, 1), 0.0)
                if r == 2:
                    value = down_one(value)
                for part, rows in halves(c, r % 2):
                    basis_ref[0, rows, tile_of(k)] += value[part]
    for r in range(2):
        for k, block in unrolled(EFF_TILE + r, EFF_TILE + 2, r):
            above = block if r == 0 else down_one(block)
            for part, rows in halves(0, r):
                eff_ref[0, rows, tile_of(k)] = block[part]
            for part, rows in halves(0, 1 - r):
                eff_ref[1, rows, tile_of(k)] = above[part]

    density = [
        jnp.sum(jnp.where(lane == 73 + r, rows_of(0, tail + 1), 0.0), 1, keepdims=True)
        for r in range(2)
    ]
    density = jnp.concatenate(
        [density[0][0:8], density[1][0:8], density[0][8:16], density[1][8:16]], 0
    )

    weight = density * math.sqrt(2.0 / HRING)
    w = [basis_ref[1, 0:32, 256 * a : 256 * a + 256] * weight for a in range(6)]
    s1, s2, d1, d2 = w[1] + w[5], w[2] + w[4], w[1] - w[5], w[2] - w[4]
    plus, minus = w[0] + w[3], w[0] - w[3]
    half = 0.5 * (s1 + s2)
    diff = 0.5 * (s1 - s2)
    real = [plus + 2.0 * half, minus + diff, plus - half, minus - 2.0 * diff]
    real += [real[2], real[1]]
    i1, i2 = -ROOT3H * (d1 + d2), -ROOT3H * (d1 - d2)
    imag = [None, i1, i2, None, -i2, -i1]
    for p in range(6):
        cosine, sine = twiddle_ref[0, p : p + 1, :], twiddle_ref[1, p : p + 1, :]
        rows = slice(32 * p, 32 * p + 32)
        re, im = real[p] * cosine, -real[p] * sine
        if imag[p] is not None:
            re, im = re + imag[p] * sine, im + imag[p] * cosine
        for k, x in ((0, re), (256, im)):
            high, low = split(x)
            xh_ref[rows, k : k + 256] = high
            xl_ref[rows, k : k + 256] = low
    high, low = xh_ref[0:192, 0:512], xl_ref[0:192, 0:512]
    coefs = mm(high, fh_ref[...]) + mm(low, fh_ref[...]) + mm(high, fl_ref[...])
    for k in range(2):
        coef_ref[256 * k : 256 * k + 192, :] = coefs[:, tile_of(k)]
        coef_ref[256 * k + 192 : 256 * k + 256, :] = jnp.zeros((64, LANES), f32)

    def place(r, k):
        return pl.ds(256 * k + 16 * (r // 16) + 8 * (r % 2) + r // 2 % 8, 8, stride=32)

    zero = jnp.zeros((8, LANES), f32)
    for k in range(2):
        lanes = tile_of(k)
        rows = [coef_ref[place(r, k), :] for r in range(NR)]
        forward, moment = zero, zero
        for r in range(NR):
            forward = rows[r] + ratio_ref[r] * forward
            moment = moment + (radius[r] ** 4 / NR) * rows[r]
            pot_ref[r, :, lanes] = forward
        chosen = (lane_index((8, LANES)) == 0) & (row_index((8, LANES)) == 2)
        moment = jnp.where(chosen, rotation_gain * moment, 0.0)
        back = zero
        for r in reversed(range(NR)):
            if r + 1 < NR:
                back = ratio_ref[r + 1] * (rows[r + 1] + back)
            pot_ref[r, :, lanes] = (
                (pot_ref[r, :, lanes] + back) * scale_ref[...] + radius[r] ** 2 * moment
            )
    for k in range(2):
        for r in range(NR):
            coef_ref[place(r, k), :] = pot_ref[r, :, tile_of(k)]

    for k in range(2):
        for p in range(6):
            x = coef_ref[256 * k + 32 * p : 256 * k + 32 * p + 32, :]
            high, low = split(x)
            rest = (x - high.astype(f32) - low.astype(f32)).astype(bf16)
            for n, piece in enumerate((high, low, rest)):
                xl_ref[64 * n + 32 * k : 64 * n + 32 * k + 32, tile_of(p)] = piece
    degrees = slots_ref[...]
    for t in range(8):
        d = degrees[t : t + 1, :]
        where_from = (d % 6) * LANES + d // 6
        pick = jnp.where(row_index((LDEG, LANES)) == where_from, 1.0, 0.0).astype(bf16)
        chosen = mm(xl_ref[0:192, 0:LDEG], pick)
        chosen = chosen[0:64] + chosen[64:128] + chosen[128:192]
        c0, c1, c2, c3 = [
            jnp.concatenate([chosen[k : k + 8], chosen[k + 16 : k + 24]], 0)
            for k in (0, 8, 32, 40)
        ]
        joined = [
            jnp.where(lane < 96, c0, pltpu.roll(c1, 96, 1)),
            jnp.where(lane < 64, pltpu.roll(c1, 96, 1), pltpu.roll(c2, 64, 1)),
            jnp.where(lane < 32, pltpu.roll(c2, 64, 1), pltpu.roll(c3, 32, 1)),
        ]
        for k, block in enumerate(joined):
            send_ref[pl.ds(MID_TILES * t + k, 16, stride=8 * MID_TILES), :] = block

    high, low = split(jnp.concatenate([coef_ref[0:192, :], coef_ref[256:448, :]], 1))
    field = mm(high, th_ref[...]) + mm(low, th_ref[...]) + mm(high, tl_ref[...])
    re, im = [], []
    for p in range(6):
        cosine, sine = twiddle_ref[0, p : p + 1, :], twiddle_ref[1, p : p + 1, :]
        x, y = field[32 * p : 32 * p + 32, 0:256], field[32 * p : 32 * p + 32, 256:512]
        re.append(x * cosine - y * sine)
        im.append(x * sine + y * cosine)
    a1, a2, e1, e2 = re[1] + re[5], re[2] + re[4], im[1] - im[5], im[2] - im[4]
    plus, minus = re[0] + re[3], re[0] - re[3]
    half, diff = 0.5 * (a1 + a2), 0.5 * (a1 - a2)
    o1, o2 = ROOT3H * (e1 + e2), ROOT3H * (e1 - e2)
    parts = [plus + 2.0 * half, minus + diff - o1, plus - half - o2, minus - 2.0 * diff,
             plus - half + o2, minus + diff + o1]
    for a in range(6):
        basis_ref[0, 0:32, 256 * a : 256 * a + 256] += gravity_gain * density * parts[a]

    idx = row_index((16, 256))
    wide_lane = lane_index((16, 256))
    after = jnp.where(idx < 8, idx + 8, jnp.where(idx == 15, -1000, idx - 7))
    before = jnp.where(idx >= 8, idx - 8, jnp.where(idx == 0, -1000, idx + 7))
    is_high = (wide_lane < 96) | ((wide_lane >= 192) & (wide_lane < 200))
    for half in range(2):
        masks = {}
        for c in range(3):
            for dr, index in ((0, idx), (1, after), (-1, before)):
                for dh in range(2):
                    base = 48 * dh + 16 * c
                    hit = (wide_lane == index + base) | (wide_lane == index + base + 96)
                    if dr == 1 - 2 * half:
                        edge = 15 if half == 0 else 0
                        beyond = 192 + 3 * dh + c
                        hit |= (idx == edge) & (
                            (wide_lane == beyond) | (wide_lane == beyond + 8)
                        )
                    masks[c, dr, dh] = jnp.where(hit, 1.0, 0.0)
        for q in range(4):
            for c in range(3):
                row, start = 4 * c + q, 48 * q + 16 * c
                block = jnp.zeros((16, 256), f32)
                for c2 in range(3):
                    for dr in range(2):
                        for dh in range(2):
                            value = stiff_ref[12 * row + 4 * c2 + 2 * dr + dh]
                            block = block + value * masks[c2, dr - q // 2, dh]
                high = block.astype(bf16)
                low = jnp.where(is_high, block - high.astype(f32), 0.0).astype(bf16)
                matrix_ref[half, start : start + 16, :] = high
                matrix_ref[half, 192 + start : 208 + start, :] = low
        xs_ref[half, 208:256, :] = jnp.zeros((48, HRING), bf16)
        halo_ref[half, 6:8, :] = jnp.zeros((2, HRING), f32)

    lane_row = lane_index((1, LANES))

    def total(x):
        return jnp.sum(jnp.sum(x, 0, keepdims=True), 1, keepdims=True)

    def spread(v):
        for dh, x in ((0, v), (1, pltpu.roll(v, HRING - 1, 1))):
            high, low = split(x)
            for c in range(3):
                for half in range(2):
                    rows = slice(32 * c + 16 * half, 32 * c + 16 * half + 16)
                    start = 48 * dh + 16 * c
                    xs_ref[half, start : start + 16, :] = high[rows]
                    xs_ref[half, 96 + start : 112 + start, :] = low[rows]
                    edge = 32 * c + 16 - half
                    halo_ref[half, 3 * dh + c : 3 * dh + c + 1, :] = x[edge : edge + 1]
        for half in range(2):
            x = halo_ref[half]
            high = x.astype(bf16).astype(f32)
            xs_ref[half, 192:208, :] = jnp.concatenate([high, x - high], 0).astype(bf16)

    first_lane = lane_index((96, 256)) == 0

    def products(n, image, j):
        cols = slice(256 * n, 256 * n + 256)
        v, before = basis_ref[j + 1, :, cols], basis_ref[j, :, cols]
        return image * v, image * image, image * before

    def apply(j):
        carry, sums = None, None
        for n in range(6):
            cols = slice(256 * n, 256 * n + 256)
            images, passes = [], []
            for half in range(2):
                rows = slice(16 * half, 16 * half + 16)
                force = mm(matrix_ref[half], xs_ref[half, :, cols])
                force = (force[0:192] + force[192:384]).reshape(4, 3, 16, 256)
                here, above = eff_ref[0, rows, cols][None], eff_ref[1, rows, cols][None]
                images.append(force[0] * here + force[2] * above)
                passes.append(force[1] * here + force[3] * above)

            def joined(parts):
                return jnp.concatenate([parts[h][c] for c in range(3) for h in range(2)], 0)

            image = joined(images)
            passed = pltpu.roll(joined(passes), 1, 1)
            if n == 0:
                image_ref[:, cols] = image + jnp.where(first_lane, 0.0, passed)
            else:
                image = image + jnp.where(first_lane, carry, passed)
                image_ref[:, cols] = image
                terms = products(n, image, j)
                sums = terms if sums is None else [x + y for x, y in zip(sums, terms)]
            carry = passed
        image = image_ref[:, 0:256] + jnp.where(first_lane, carry, 0.0)
        image_ref[:, 0:256] = image
        return [total(x + y) for x, y in zip(sums, products(0, image, j))]

    def inverted(x):
        return jnp.where(x > 0.0, 1.0 / x, 0.0)

    def root(x):
        return jnp.where(x > 0.0, x * lax.rsqrt(x), 0.0)

    spread(basis_ref[1])
    load_norm = total(basis_ref[0] * basis_ref[0])
    _, image_norm, cross = apply(0)
    rough = jnp.maximum(image_norm - 2.0 * cross + load_norm, 1e-6 * (image_norm + load_norm))
    scale = jnp.where(rough > 0.0, lax.rsqrt(rough), 0.0)

    def step(j, state):
        moments, a, b, scale, norm_before = state
        v = scale * (image_ref[...] - a * basis_ref[j] - b * basis_ref[j - 1])
        basis_ref[j + 1] = v
        leaving(j).start()
        norm = total(v * v)
        spread(v)
        inner, image_norm, cross = apply(j)
        inverse = inverted(norm)
        a = inner * inverse
        b = jnp.where(j == 1, 0.0, cross * inverted(norm_before))
        beside = root(norm) * inverted(jnp.abs(scale) * root(norm_before))
        moments = (
            moments
            + jnp.where(lane_row == j - 1, a, 0.0)
            + jnp.where(lane_row == jnp.where(j == 1, 16, 6 + j), beside, 0.0)
            + jnp.where(lane_row == 23 + j, root(inverse), 0.0)
        )
        rough = jnp.maximum(image_norm - a * inner - b * cross, 1e-6 * image_norm)
        scale = jnp.where(rough > 0.0, lax.rsqrt(rough), 0.0)
        return moments, a, b, scale, norm

    one = jnp.ones((1, 1), f32)
    moments = lax.fori_loop(
        1, 7, step, (jnp.zeros((1, LANES), f32), 0.0 * one, one, -scale, one)
    )[0]
    send_ref[pl.ds(3, LANES, stride=MID_TILES), :] = jnp.broadcast_to(moments, (LANES, LANES))
    for slot in range(7):
        leaving(slot).wait()


def solve_kernel(place_ref, moments_ref, kept_ref, out_ref, x_ref, basis_ref, sems):
    def arriving(slot):
        return pltpu.make_async_copy(kept_ref.at[slot], basis_ref.at[slot], sems.at[slot])

    for slot in range(7):
        arriving(slot).start()
    table = jnp.transpose(moments_ref[pl.ds(3, LANES, stride=MID_TILES), :])
    diagonal, beside, start = table[0:8], table[8:16], table[16:17]
    first = row_index((8, LANES)) == 0
    residual = jnp.where(first, start, 0.0)

    def total(x):
        return jnp.sum(jnp.sum(x, 0, keepdims=True), 1, keepdims=True)

    def applied(v):
        return (
            diagonal * v
            + beside * pltpu.roll(v, 7, 0)
            + pltpu.roll(beside * v, 1, 0)
        )

    image = applied(residual)
    norm, product = total(residual * residual), total(residual * image)
    size = norm / product
    direction, along, y = residual, image, size * residual
    for i in range(5):
        residual = residual - size * along
        image = applied(residual)
        new, product = total(residual * residual), total(residual * image)
        growth = new / norm
        size = new / (product - growth * new / size)
        direction, along = residual + growth * direction, image + growth * along
        y, norm = y + size * direction, new
    mine = lane_index((8, LANES)) == place_ref[0]
    own = jnp.sum(jnp.where(mine, y * table[24:32], 0.0), 1, keepdims=True)
    for group in ((0, 1, 2), (3, 4), (5, 6)):
        for slot in group:
            arriving(slot).wait()
        x = basis_ref[0] if group[0] == 0 else x_ref[...]
        for slot in group:
            if slot:
                x = x + own[slot - 1 : slot, :] * basis_ref[slot]
        x_ref[...] = x

    lane = lane_index((16, LANES))

    def node_rows(c, r, k):
        start = 32 * c + 8 * (r % 2)
        block = jnp.concatenate(
            [x_ref[start : start + 8, tile_of(k)], x_ref[start + 16 : start + 24, tile_of(k)]], 0
        )
        return up_one(block) if r == 2 else block

    def at(t, tile):
        return pl.ds(OUT_TILES * t + tile, 16, stride=8 * OUT_TILES)

    for u in range(4):
        even, odd = 2 * u, 2 * u + 1
        for c in range(3):
            for r in range(3):
                out_ref[at(even, 4 * c + r), :] = node_rows(c, r, 3 * u)
                out_ref[at(odd, 4 * c + r), :] = node_rows(c, r, 3 * u + 2)
            low, high = node_rows(c, 0, 3 * u + 1), node_rows(c, 1, 3 * u + 1)
            out_ref[at(even, 4 * c + 3), :] = jnp.where(lane < 64, low, pltpu.roll(high, 64, 1))
            out_ref[at(odd, 4 * c + 3), :] = jnp.where(lane < 64, pltpu.roll(low, 64, 1), high)
        extra = [node_rows(c, 2, 3 * u + 1) for c in range(3)]
        out_ref[at(even, OUT_TAIL), :] = jnp.where(
            lane < 64, extra[0], pltpu.roll(extra[1], 64, 1)
        )
        out_ref[at(odd, OUT_TAIL), :] = jnp.where(
            lane < 64, pltpu.roll(extra[0], 64, 1), extra[1]
        )
        for parity, rows in ((0, even), (1, odd)):
            block = extra[2] if parity == 0 else pltpu.roll(extra[2], 64, 1)
            following = (2 * u + parity + 1) % 8
            k, source = 3 * (following // 2) + following % 2, 64 * (following % 2)
            for c in range(3):
                for r in range(3):
                    target = 64 + 3 * c + r
                    value = pltpu.roll(node_rows(c, r, k), (target - source) % LANES, 1)
                    block = jnp.where(lane == target, value, block)
            out_ref[at(rows, OUT_TAIL + 1), :] = block


def finish_kernel(parity_ref, stiff_ref, recv_ref, stress_ref, shear_far_ref, relax_far_ref,
                  x_out_ref, stress_out_ref, x_ref, new_ref, matrix_ref, shear_ref, relax_ref,
                  first_ref, x_sems, sems):
    shear_arriving = pltpu.make_async_copy(shear_far_ref, shear_ref, sems.at[3])
    relax_arriving = pltpu.make_async_copy(relax_far_ref, relax_ref, sems.at[4])
    shear_arriving.start()
    relax_arriving.start()
    parity = parity_ref[0]
    wide = pl.ds(pl.multiple_of(64 * parity, 64), 128)
    narrow = pl.ds(pl.multiple_of(128 * (1 - parity), 64), 64)

    def block(k):
        return jnp.transpose(recv_ref[pl.ds(k, LANES, stride=OUT_TILES), :])

    def x_leaving(c):
        return pltpu.make_async_copy(x_ref.at[c, 0:2, 0:COLS], x_out_ref.at[c], x_sems.at[c])

    def leaving(part):
        rows = pl.ds(64 * part, 64)
        return pltpu.make_async_copy(
            new_ref.at[:, :, rows], stress_out_ref.at[:, :, rows], sems.at[part]
        )

    for c in range(3):
        for r in range(3):
            x_ref[c, r, wide, :] = block(4 * c + r)
        rest = block(4 * c + 3)
        x_ref[c, 0, narrow, :] = rest[0:64]
        x_ref[c, 1, narrow, :] = rest[64:128]
        x_leaving(c).start()
    rest = block(OUT_TAIL)
    x_ref[0, 2, narrow, :] = rest[0:64]
    x_ref[1, 2, narrow, :] = rest[64:128]
    rest = block(OUT_TAIL + 1)
    x_ref[2, 2, narrow, :] = rest[0:64]
    for c in range(3):
        for r in range(3):
            x_ref[c, r, COLS : COLS + 1, :] = rest[64 + 3 * c + r : 65 + 3 * c + r]

    lane = lane_index((16, 192))
    same = (lane % 16) == row_index((16, 192))
    for a in range(12):
        line = jnp.zeros((16, 192), f32)
        for b in range(12):
            line = jnp.where(lane // 16 == b, stiff_ref[12 * a + b], line)
        high, low = split(jnp.where(same, line, 0.0))
        for k, piece in enumerate((high, high, low)):
            matrix_ref[16 * a : 16 * a + 16, 256 * k : 256 * k + 192] = piece
            matrix_ref[16 * a : 16 * a + 16, 256 * k + 192 : 256 * k + 256] = jnp.zeros(
                (16, 64), bf16
            )

    pad = jnp.zeros((64, 2 * LANES), bf16)

    def forces(n):
        corners = []
        for c in range(3):
            for dr in range(2):
                for dh in range(2):
                    span = slice(16 * n + dh, 16 * n + dh + 16)
                    corners.append(
                        jnp.concatenate([x_ref[c, dr, span, :], x_ref[c, 1 + dr, span, :]], 1)
                    )
        high, low = split(jnp.concatenate(corners, 0))
        return mm(matrix_ref[...], jnp.concatenate([high, pad, low, pad, high, pad], 0))

    def store(n, force):
        rows = slice(16 * n, 16 * n + 16)
        for r in range(2):
            relax = relax_ref[r, rows, :]
            share = 1.0 / (1.0 + 0.5 * relax)
            eff, kept = shear_ref[r, rows, :] * share, (1.0 - 0.5 * relax) * share
            for a in range(12):
                new_ref[a, r, rows, :] = (
                    kept * stress_ref[a, r, rows, :]
                    + eff * force[16 * a : 16 * a + 16, tile_of(r)]
                )

    for n in range(4):
        first_ref[n] = forces(n)
    shear_arriving.wait()
    relax_arriving.wait()
    for n in range(4):
        store(n, first_ref[n])
    leaving(0).start()
    for n in range(4, COLS // 16):
        store(n, forces(n))
        if n % 4 == 3:
            leaving(n // 4).start()
    for c in range(3):
        x_leaving(c).wait()
    for part in range(3):
        leaving(part).wait()


def potential_kernel(recv_ref, out_ref):
    blocks = [jnp.transpose(recv_ref[pl.ds(k, LANES, stride=MID_TILES), :]) for k in range(3)]
    lines = jnp.concatenate(blocks, 0)
    for part in range(2):
        for r in range(2):
            start = 96 * (2 * part + r)
            out_ref[:, r, tile_of(part)] = lines[start : start + 96]


def whole(shape):
    return pl.BlockSpec(shape, lambda *_: (0,) * len(shape))


smem = pl.BlockSpec(memory_space=pltpu.SMEM)


def far_memory(x):
    return pltpu.with_memory_space_constraint(x, pltpu.HBM)


def exchanged(lines):
    count = lines.shape[0]
    rows = lines.reshape(LANES, 1, count)
    return lax.all_to_all(rows, ALL, 0, 0, tiled=True).reshape(count, LANES)


def params(mib):
    return pltpu.CompilerParams(vmem_limit_bytes=mib * 2**20)


def body(load, previous, stress_old, shear_modulus, relaxation, density_jump, element_stiffness,
         degree_slots):
    tile_place = lax.axis_index(TILE)
    place = (lax.axis_index(CAP) * 8 + tile_place).astype(jnp.int32).reshape(1)
    parity = (tile_place % 2).astype(jnp.int32).reshape(1)
    stiff = element_stiffness.reshape(144)
    slots = jnp.pad(degree_slots.reshape(8, 96), ((0, 0), (0, 32)), constant_values=-1)
    (fh, fl), (th, tl), twiddle = transform_tables()
    ratio, scale, radius = radial_tables()

    one = pl.BlockSpec((1, 2, COLS, LANES), lambda c: (c, 0, 0, 0))
    four = pl.BlockSpec((4, 2, COLS, LANES), lambda c: (c, 0, 0, 0))
    field = whole((2, COLS, LANES))
    packed = pl.pallas_call(
        pack_kernel,
        grid=(3,),
        in_specs=[smem, smem, one, one, four, field, field],
        out_specs=whole((IN_TILES * LANES, LANES)),
        out_shape=pltpu.HBM((IN_TILES * LANES, LANES), f32),
        scratch_shapes=[pltpu.VMEM((3, COLS, LANES), f32), pltpu.VMEM((256, LANES), f32)],
        compiler_params=params(12),
    )(parity, *[far_memory(x) for x in (density_jump, load, previous, stress_old, shear_modulus, relaxation)])
    received = exchanged(packed)

    basis, sent = pl.pallas_call(
        functools.partial(section_kernel, radius=[float(x) for x in radius]),
        in_specs=[smem] + [pl.BlockSpec(memory_space=pltpu.VMEM)] * 9,
        out_specs=[pl.BlockSpec(memory_space=pl.ANY), pl.BlockSpec(memory_space=pltpu.VMEM)],
        out_shape=[
            pltpu.HBM((7, 96, HRING), f32),
            pltpu.HBM((MID_TILES * LANES, LANES), f32),
        ],
        scratch_shapes=[
            pltpu.VMEM((8, 96, HRING), f32),
            pltpu.SemaphoreType.DMA((7,)),
            pltpu.VMEM((2, 32, HRING), f32),
            pltpu.VMEM((2, 384, 256), bf16),
            pltpu.VMEM((192, LDEG), bf16),
            pltpu.VMEM((192, LDEG), bf16),
            pltpu.VMEM((2, 256, HRING), bf16),
            pltpu.VMEM((2, 8, HRING), f32),
            pltpu.VMEM((96, HRING), f32),
            pltpu.VMEM((512, LANES), f32),
            pltpu.VMEM((NR, 8, 256), f32),
        ],
        compiler_params=params(20),
    )(stiff, received, slots, fh, fl, th, tl, twiddle, ratio, scale)
    shared = exchanged(sent)

    back = pl.pallas_call(
        solve_kernel,
        grid=(1,),
        in_specs=[
            smem,
            whole((MID_TILES * LANES, LANES)),
            pl.BlockSpec(memory_space=pl.ANY),
        ],
        out_specs=whole((OUT_TILES * LANES, LANES)),
        out_shape=pltpu.HBM((OUT_TILES * LANES, LANES), f32),
        scratch_shapes=[
            pltpu.VMEM((96, HRING), f32),
            pltpu.VMEM((7, 96, HRING), f32),
            pltpu.SemaphoreType.DMA((7,)),
        ],
        compiler_params=params(12),
    )(place, shared, far_memory(basis))
    returned = exchanged(back)

    potential = pl.pallas_call(
        potential_kernel,
        grid=(1,),
        in_specs=[whole((MID_TILES * LANES, LANES))],
        out_specs=whole((96, 2, 256)),
        out_shape=jax.ShapeDtypeStruct((96, 2, 256), f32),
        compiler_params=params(4),
    )(shared)

    displacement, stress_new = pl.pallas_call(
        finish_kernel,
        in_specs=[smem, smem]
        + [pl.BlockSpec(memory_space=pltpu.VMEM)] * 2
        + [pl.BlockSpec(memory_space=pl.ANY)] * 2,
        out_specs=[pl.BlockSpec(memory_space=pl.ANY)] * 2,
        out_shape=[
            jax.ShapeDtypeStruct((3, 2, COLS, LANES), f32),
            jax.ShapeDtypeStruct((12, 2, COLS, LANES), f32),
        ],
        scratch_shapes=[
            pltpu.VMEM((3, 3, COLS + 8, LANES), f32),
            pltpu.VMEM((12, 2, COLS, LANES), f32),
            pltpu.VMEM((192, 768), bf16),
            pltpu.VMEM((2, COLS, LANES), f32),
            pltpu.VMEM((2, COLS, LANES), f32),
            pltpu.VMEM((4, COLS, 2 * LANES), f32),
            pltpu.SemaphoreType.DMA((3,)),
            pltpu.SemaphoreType.DMA((5,)),
        ],
        compiler_params=params(12),
    )(parity, stiff, returned, stress_old, far_memory(shear_modulus), far_memory(relaxation))
    return displacement, stress_new, potential


def solution(mesh):
    torus = Mesh(mesh.devices.reshape(4, 4, 4, 2), ("cap_0", "cap_1", "tile_0", "tile_1"))
    return jax.shard_map(
        body,
        mesh=torus,
        in_specs=(
            P(None, CAP, TILE, None),
            P(None, CAP, TILE, None),
            P(None, CAP, TILE, None),
            P(CAP, TILE, None),
            P(CAP, TILE, None),
            P(CAP),
            P(),
            P(),
        ),
        out_specs=(P(None, CAP, TILE, None), P(None, CAP, TILE, None), P(TILE, CAP, None)),
        check_vma=False,
    )
```

```python
import functools
import math

import jax
import jax.numpy as jnp
import ml_dtypes
import numpy as np
from jax import lax
from jax.experimental import pallas as pl
from jax.experimental.pallas import tpu as pltpu
from jax.sharding import Mesh
from jax.sharding import PartitionSpec as P

HRING = 1536
LDEG = 768
NR = 32
TILE = ("tile_0", "tile_1")
CAP = ("cap_0", "cap_1")
ALL = ("cap_0", "cap_1", "tile_0", "tile_1")
LANES = 128
COLS = 192
ROOT3H = math.sqrt(3.0) / 2.0
rotation_gain = 2.0
gravity_gain = 0.2

EFF_TILE = 21
TAIL_TILE = 24
IN_TILES = 26
MID_TILES = 4
OUT_TAIL = 12
OUT_TILES = 14

f32 = jnp.float32
bf16 = jnp.bfloat16


def split_table(table):
    high = table.astype(ml_dtypes.bfloat16)
    low = (table - high.astype(np.float64)).astype(ml_dtypes.bfloat16)
    return high, low


def transform_tables():
    q = np.arange(128)[None, :]
    b = np.arange(256)[:, None]
    angle = 2.0 * np.pi * ((q * b) % 256) / 256.0
    cosine, sine = np.cos(angle), np.sin(angle)
    table = np.concatenate(
        [np.concatenate([cosine, sine], 1), np.concatenate([sine, -cosine], 1)], 0
    )
    p = np.arange(8)[:, None]
    turn = 2.0 * np.pi * ((p * np.arange(256)[None, :]) % HRING) / HRING
    twiddle = np.stack([np.cos(turn), np.sin(turn)]).astype(np.float32)
    return split_table(table), split_table(np.ascontiguousarray(table.T)), twiddle


def radial_tables():
    radius = 1.0 - 0.45 * (np.arange(NR) + 0.5) / NR
    degree = 6.0 * np.arange(128)[None, :] + np.arange(8)[:, None]
    log_radius = np.log(radius)
    ratio = np.zeros((NR, 8, 128))
    for r in range(1, NR):
        ratio[r] = np.exp(-degree * (log_radius[r - 1] - log_radius[r]))
    scale = 1.0 / np.sqrt(2.0 * degree + 1.0)
    return ratio.astype(np.float32), scale.astype(np.float32), radius


def split(x):
    high = x.astype(bf16)
    return high, (x - high.astype(f32)).astype(bf16)


def mm(a, b):
    return jnp.dot(a, b, preferred_element_type=f32)


def lane_index(shape):
    return lax.broadcasted_iota(jnp.int32, shape, len(shape) - 1)


def row_index(shape):
    return lax.broadcasted_iota(jnp.int32, shape, 0)


def tile_of(k):
    return slice(k * LANES, (k + 1) * LANES)


def down_one(x):
    return jnp.where(row_index(x.shape) == 0, 0.0, pltpu.roll(x, 1, 0))


def up_one(x):
    n = x.shape[0]
    return jnp.where(row_index(x.shape) == n - 1, 0.0, pltpu.roll(x, n - 1, 0))


def pack_kernel(parity_ref, density_ref, load_far, prev_far, stress_far, shear_far, relax_far,
                out_ref, load_ref, prev_ref, stress_ref, shear_ref, relax_ref, acc_ref, tail_ref,
                sems):
    parity = parity_ref[0]
    wide = pl.ds(pl.multiple_of(64 * parity, 64), 128)
    narrow = pl.ds(pl.multiple_of(128 * (1 - parity), 64), 64)
    copies = [
        pltpu.make_async_copy(relax_far, relax_ref, sems.at[0]),
        pltpu.make_async_copy(shear_far, shear_ref, sems.at[1]),
    ]
    for comp in range(3):
        four = pl.ds(4 * comp, 4)
        for far, near in (
            (prev_far.at[comp], prev_ref.at[comp]),
            (stress_far.at[four], stress_ref.at[four]),
            (load_far.at[comp], load_ref.at[comp]),
        ):
            copies.append(pltpu.make_async_copy(far, near, sems.at[len(copies)]))
    for copy in copies:
        copy.start()

    def put(tile, block):
        out_ref[pl.ds(tile, LANES, stride=IN_TILES), :] = jnp.transpose(block)

    copies[0].wait()
    copies[1].wait()
    acc_ref[:2] = shear_ref[...] / (1.0 + 0.5 * relax_ref[...])
    put(EFF_TILE, acc_ref[0, wide, :])
    put(EFF_TILE + 1, acc_ref[1, wide, :])
    put(EFF_TILE + 2, jnp.concatenate([acc_ref[0, narrow, :], acc_ref[1, narrow, :]], 0))
    tail_ref[192:256, :] = jnp.zeros((64, LANES), f32)
    for r in range(2):
        tail_ref[201 + r : 202 + r, :] = jnp.full((1, LANES), density_ref[r], f32)

    for comp in range(3):
        base = comp * 7
        copies[2 + 3 * comp].wait()
        put(base, prev_ref[comp, 0, wide, :])
        put(base + 1, prev_ref[comp, 1, wide, :])
        rest = [prev_ref[comp, r, narrow, :] for r in range(2)]
        put(base + 2, jnp.concatenate(rest, 0))

        copies[3 + 3 * comp].wait()
        copies[4 + 3 * comp].wait()
        relax = relax_ref[...]
        carried = relax / (1.0 + 0.5 * relax)
        part = [
            [carried[r] * stress_ref[4 * comp + q, r] for r in range(2)] for q in range(4)
        ]
        near = [part[0][0], part[0][1] + part[2][0], part[2][1]]
        far = [part[1][0], part[1][1] + part[3][0], part[3][1]]
        for r in range(3):
            total = near[r] + down_one(far[r])
            if r < 2:
                total = total + load_ref[comp, r]
            acc_ref[r] = total
            place = 192 + 3 * comp + r
            tail_ref[place : place + 1, :] = far[r][COLS - 1 : COLS, :]
        for r in range(3):
            put(base + 3 + r, acc_ref[r, wide, :])
        put(base + 6, jnp.concatenate([acc_ref[0, narrow, :], acc_ref[1, narrow, :]], 0))
        tail_ref[64 * comp : 64 * comp + 64, :] = acc_ref[2, narrow, :]

    put(TAIL_TILE, tail_ref[:128, :])
    put(TAIL_TILE + 1, tail_ref[128:, :])


def section_kernel(stiff_ref, recv_ref, slots_ref, fh_ref, fl_ref, th_ref, tl_ref, twiddle_ref,
                   ratio_ref, scale_ref, kept_ref, send_ref, basis_ref, sems,
                   eff_ref, matrix_ref, xh_ref, xl_ref, xs_ref, halo_ref, image_ref, coef_ref, pot_ref,
                   *, radius):
    lane = lane_index((16, LANES))

    def leaving(slot):
        return pltpu.make_async_copy(basis_ref.at[slot + 1], kept_ref.at[slot], sems.at[slot])

    def rows_of(t, tile):
        return recv_ref[pl.ds(IN_TILES * t + tile, 16, stride=8 * IN_TILES), :]

    def unrolled(wide_tile, narrow_tile, half):
        for u in range(4):
            even, odd = rows_of(2 * u, narrow_tile), rows_of(2 * u + 1, narrow_tile)
            if half == 0:
                middle = jnp.where(lane < 64, even, pltpu.roll(odd, 64, 1))
            else:
                middle = jnp.where(lane < 64, pltpu.roll(even, 64, 1), odd)
            yield 3 * u, rows_of(2 * u, wide_tile)
            yield 3 * u + 1, middle
            yield 3 * u + 2, rows_of(2 * u + 1, wide_tile)

    tail = TAIL_TILE

    def halves(c, r):
        for h in range(2):
            yield slice(8 * h, 8 * h + 8), slice(32 * c + 16 * h + 8 * r, 32 * c + 16 * h + 8 * r + 8)

    for c in range(3):
        for r in range(2):
            for k, block in unrolled(7 * c + r, 7 * c + 2, r):
                for part, rows in halves(c, r):
                    basis_ref[1, rows, tile_of(k)] = block[part]
            for k, block in unrolled(7 * c + 3 + r, 7 * c + 6, r):
                for part, rows in halves(c, r):
                    basis_ref[0, rows, tile_of(k)] = block[part]
        for k, block in unrolled(7 * c + 5, tail + c // 2, c % 2):
            block = down_one(block)
            for part, rows in halves(c, 0):
                basis_ref[0, rows, tile_of(k)] += block[part]
    leaving(0).start()
    for t in range(8):
        following = (t + 1) % 8
        k, target = 3 * (following // 2) + following % 2, 64 * (following % 2)
        block = rows_of(t, tail + 1)
        for c in range(3):
            for r in range(3):
                shift = (target - 64 - 3 * c - r) % LANES
                value = jnp.where(lane == target, pltpu.roll(block, shift, 1), 0.0)
                if r == 2:
                    value = down_one(value)
                for part, rows in halves(c, r % 2):
                    basis_ref[0, rows, tile_of(k)] += value[part]
    for r in range(2):
        for k, block in unrolled(EFF_TILE + r, EFF_TILE + 2, r):
            above = block if r == 0 else down_one(block)
            for part, rows in halves(0, r):
                eff_ref[0, rows, tile_of(k)] = block[part]
            for part, rows in halves(0, 1 - r):
                eff_ref[1, rows, tile_of(k)] = above[part]

    density = [
        jnp.sum(jnp.where(lane == 73 + r, rows_of(0, tail + 1), 0.0), 1, keepdims=True)
        for r in range(2)
    ]
    density = jnp.concatenate(
        [density[0][0:8], density[1][0:8], density[0][8:16], density[1][8:16]], 0
    )

    weight = density * math.sqrt(2.0 / HRING)
    w = [basis_ref[1, 0:32, 256 * a : 256 * a + 256] * weight for a in range(6)]
    s1, s2, d1, d2 = w[1] + w[5], w[2] + w[4], w[1] - w[5], w[2] - w[4]
    plus, minus = w[0] + w[3], w[0] - w[3]
    half = 0.5 * (s1 + s2)
    diff = 0.5 * (s1 - s2)
    real = [plus + 2.0 * half, minus + diff, plus - half, minus - 2.0 * diff]
    real += [real[2], real[1]]
    i1, i2 = -ROOT3H * (d1 + d2), -ROOT3H * (d1 - d2)
    imag = [None, i1, i2, None, -i2, -i1]
    for p in range(6):
        cosine, sine = twiddle_ref[0, p : p + 1, :], twiddle_ref[1, p : p + 1, :]
        rows = slice(32 * p, 32 * p + 32)
        re, im = real[p] * cosine, -real[p] * sine
        if imag[p] is not None:
            re, im = re + imag[p] * sine, im + imag[p] * cosine
        for k, x in ((0, re), (256, im)):
            high, low = split(x)
            xh_ref[rows, k : k + 256] = high
            xl_ref[rows, k : k + 256] = low
    high, low = xh_ref[0:192, 0:512], xl_ref[0:192, 0:512]
    coefs = mm(high, fh_ref[...]) + mm(low, fh_ref[...]) + mm(high, fl_ref[...])
    for k in range(2):
        coef_ref[256 * k : 256 * k + 192, :] = coefs[:, tile_of(k)]
        coef_ref[256 * k + 192 : 256 * k + 256, :] = jnp.zeros((64, LANES), f32)

    def place(r, k):
        return pl.ds(256 * k + 16 * (r // 16) + 8 * (r % 2) + r // 2 % 8, 8, stride=32)

    zero = jnp.zeros((8, LANES), f32)
    for k in range(2):
        lanes = tile_of(k)
        rows = [coef_ref[place(r, k), :] for r in range(NR)]
        forward, moment = zero, zero
        for r in range(NR):
            forward = rows[r] + ratio_ref[r] * forward
            moment = moment + (radius[r] ** 4 / NR) * rows[r]
            pot_ref[r, :, lanes] = forward
        chosen = (lane_index((8, LANES)) == 0) & (row_index((8, LANES)) == 2)
        moment = jnp.where(chosen, rotation_gain * moment, 0.0)
        back = zero
        for r in reversed(range(NR)):
            if r + 1 < NR:
                back = ratio_ref[r + 1] * (rows[r + 1] + back)
            pot_ref[r, :, lanes] = (
                (pot_ref[r, :, lanes] + back) * scale_ref[...] + radius[r] ** 2 * moment
            )
    for k in range(2):
        for r in range(NR):
            coef_ref[place(r, k), :] = pot_ref[r, :, tile_of(k)]

    for k in range(2):
        for p in range(6):
            x = coef_ref[256 * k + 32 * p : 256 * k + 32 * p + 32, :]
            high, low = split(x)
            rest = (x - high.astype(f32) - low.astype(f32)).astype(bf16)
            for n, piece in enumerate((high, low, rest)):
                xl_ref[64 * n + 32 * k : 64 * n + 32 * k + 32, tile_of(p)] = piece
    degrees = slots_ref[...]
    for t in range(8):
        d = degrees[t : t + 1, :]
        where_from = (d % 6) * LANES + d // 6
        pick = jnp.where(row_index((LDEG, LANES)) == where_from, 1.0, 0.0).astype(bf16)
        chosen = mm(xl_ref[0:192, 0:LDEG], pick)
        chosen = chosen[0:64] + chosen[64:128] + chosen[128:192]
        c0, c1, c2, c3 = [
            jnp.concatenate([chosen[k : k + 8], chosen[k + 16 : k + 24]], 0)
            for k in (0, 8, 32, 40)
        ]
        joined = [
            jnp.where(lane < 96, c0, pltpu.roll(c1, 96, 1)),
            jnp.where(lane < 64, pltpu.roll(c1, 96, 1), pltpu.roll(c2, 64, 1)),
            jnp.where(lane < 32, pltpu.roll(c2, 64, 1), pltpu.roll(c3, 32, 1)),
        ]
        for k, block in enumerate(joined):
            send_ref[pl.ds(MID_TILES * t + k, 16, stride=8 * MID_TILES), :] = block

    high, low = split(jnp.concatenate([coef_ref[0:192, :], coef_ref[256:448, :]], 1))
    field = mm(high, th_ref[...]) + mm(low, th_ref[...]) + mm(high, tl_ref[...])
    re, im = [], []
    for p in range(6):
        cosine, sine = twiddle_ref[0, p : p + 1, :], twiddle_ref[1, p : p + 1, :]
        x, y = field[32 * p : 32 * p + 32, 0:256], field[32 * p : 32 * p + 32, 256:512]
        re.append(x * cosine - y * sine)
        im.append(x * sine + y * cosine)
    a1, a2, e1, e2 = re[1] + re[5], re[2] + re[4], im[1] - im[5], im[2] - im[4]
    plus, minus = re[0] + re[3], re[0] - re[3]
    half, diff = 0.5 * (a1 + a2), 0.5 * (a1 - a2)
    o1, o2 = ROOT3H * (e1 + e2), ROOT3H * (e1 - e2)
    parts = [plus + 2.0 * half, minus + diff - o1, plus - half - o2, minus - 2.0 * diff,
             plus - half + o2, minus + diff + o1]
    for a in range(6):
        basis_ref[0, 0:32, 256 * a : 256 * a + 256] += gravity_gain * density * parts[a]

    idx = row_index((16, 256))
    wide_lane = lane_index((16, 256))
    after = jnp.where(idx < 8, idx + 8, jnp.where(idx == 15, -1000, idx - 7))
    before = jnp.where(idx >= 8, idx - 8, jnp.where(idx == 0, -1000, idx + 7))
    is_high = (wide_lane < 96) | ((wide_lane >= 192) & (wide_lane < 200))
    for half in range(2):
        masks = {}
        for c in range(3):
            for dr, index in ((0, idx), (1, after), (-1, before)):
                for dh in range(2):
                    base = 48 * dh + 16 * c
                    hit = (wide_lane == index + base) | (wide_lane == index + base + 96)
                    if dr == 1 - 2 * half:
                        edge = 15 if half == 0 else 0
                        beyond = 192 + 3 * dh + c
                        hit |= (idx == edge) & (
                            (wide_lane == beyond) | (wide_lane == beyond + 8)
                        )
                    masks[c, dr, dh] = jnp.where(hit, 1.0, 0.0)
        for q in range(4):
            for c in range(3):
                row, start = 4 * c + q, 48 * q + 16 * c
                block = jnp.zeros((16, 256), f32)
                for c2 in range(3):
                    for dr in range(2):
                        for dh in range(2):
                            value = stiff_ref[12 * row + 4 * c2 + 2 * dr + dh]
                            block = block + value * masks[c2, dr - q // 2, dh]
                high = block.astype(bf16)
                low = jnp.where(is_high, block - high.astype(f32), 0.0).astype(bf16)
                matrix_ref[half, start : start + 16, :] = high
                matrix_ref[half, 192 + start : 208 + start, :] = low
        xs_ref[half, 208:256, :] = jnp.zeros((48, HRING), bf16)
        halo_ref[half, 6:8, :] = jnp.zeros((2, HRING), f32)

    lane_row = lane_index((1, LANES))

    def total(x):
        return jnp.sum(jnp.sum(x, 0, keepdims=True), 1, keepdims=True)

    def spread(v):
        for dh, x in ((0, v), (1, pltpu.roll(v, HRING - 1, 1))):
            high, low = split(x)
            for c in range(3):
                for half in range(2):
                    rows = slice(32 * c + 16 * half, 32 * c + 16 * half + 16)
                    start = 48 * dh + 16 * c
                    xs_ref[half, start : start + 16, :] = high[rows]
                    xs_ref[half, 96 + start : 112 + start, :] = low[rows]
                    edge = 32 * c + 16 - half
                    halo_ref[half, 3 * dh + c : 3 * dh + c + 1, :] = x[edge : edge + 1]
        for half in range(2):
            x = halo_ref[half]
            high = x.astype(bf16).astype(f32)
            xs_ref[half, 192:208, :] = jnp.concatenate([high, x - high], 0).astype(bf16)

    first_lane = lane_index((96, 256)) == 0

    def products(n, image, j):
        cols = slice(256 * n, 256 * n + 256)
        v, before = basis_ref[j + 1, :, cols], basis_ref[j, :, cols]
        return image * v, image * image, image * before

    def apply(j):
        carry, sums = None, None
        for n in range(6):
            cols = slice(256 * n, 256 * n + 256)
            images, passes = [], []
            for half in range(2):
                rows = slice(16 * half, 16 * half + 16)
                force = mm(matrix_ref[half], xs_ref[half, :, cols])
                force = (force[0:192] + force[192:384]).reshape(4, 3, 16, 256)
                here, above = eff_ref[0, rows, cols][None], eff_ref[1, rows, cols][None]
                images.append(force[0] * here + force[2] * above)
                passes.append(force[1] * here + force[3] * above)

            def joined(parts):
                return jnp.concatenate([parts[h][c] for c in range(3) for h in range(2)], 0)

            image = joined(images)
            passed = pltpu.roll(joined(passes), 1, 1)
            if n == 0:
                image_ref[:, cols] = image + jnp.where(first_lane, 0.0, passed)
            else:
                image = image + jnp.where(first_lane, carry, passed)
                image_ref[:, cols] = image
                terms = products(n, image, j)
                sums = terms if sums is None else [x + y for x, y in zip(sums, terms)]
            carry = passed
        image = image_ref[:, 0:256] + jnp.where(first_lane, carry, 0.0)
        image_ref[:, 0:256] = image
        return [total(x + y) for x, y in zip(sums, products(0, image, j))]

    def inverted(x):
        return jnp.where(x > 0.0, 1.0 / x, 0.0)

    def root(x):
        return jnp.where(x > 0.0, x * lax.rsqrt(x), 0.0)

    spread(basis_ref[1])
    load_norm = total(basis_ref[0] * basis_ref[0])
    _, image_norm, cross = apply(0)
    rough = jnp.maximum(image_norm - 2.0 * cross + load_norm, 1e-6 * (image_norm + load_norm))
    scale = jnp.where(rough > 0.0, lax.rsqrt(rough), 0.0)

    def step(j, state):
        moments, a, b, scale, norm_before = state
        v = scale * (image_ref[...] - a * basis_ref[j] - b * basis_ref[j - 1])
        basis_ref[j + 1] = v
        leaving(j).start()
        norm = total(v * v)
        spread(v)
        inner, image_norm, cross = apply(j)
        inverse = inverted(norm)
        a = inner * inverse
        b = jnp.where(j == 1, 0.0, cross * inverted(norm_before))
        beside = root(norm) * inverted(jnp.abs(scale) * root(norm_before))
        moments = (
            moments
            + jnp.where(lane_row == j - 1, a, 0.0)
            + jnp.where(lane_row == jnp.where(j == 1, 16, 6 + j), beside, 0.0)
            + jnp.where(lane_row == 23 + j, root(inverse), 0.0)
        )
        rough = jnp.maximum(image_norm - a * inner - b * cross, 1e-6 * image_norm)
        scale = jnp.where(rough > 0.0, lax.rsqrt(rough), 0.0)
        return moments, a, b, scale, norm

    one = jnp.ones((1, 1), f32)
    moments = lax.fori_loop(
        1, 7, step, (jnp.zeros((1, LANES), f32), 0.0 * one, one, -scale, one)
    )[0]
    send_ref[pl.ds(3, LANES, stride=MID_TILES), :] = jnp.broadcast_to(moments, (LANES, LANES))
    for slot in range(7):
        leaving(slot).wait()


def solve_kernel(place_ref, moments_ref, kept_ref, out_ref, x_ref, basis_ref, packed_ref, sems,
                 out_sems):
    def arriving(slot, half):
        return pltpu.make_async_copy(
            kept_ref.at[slot, :, half], basis_ref.at[slot, :, half], sems.at[half, slot]
        )

    for half in (1, 0):
        for slot in range(7):
            arriving(slot, half).start()
    table = jnp.transpose(moments_ref[pl.ds(3, LANES, stride=MID_TILES), :])
    diagonal, beside, start = table[0:8], table[8:16], table[16:17]
    first = row_index((8, LANES)) == 0
    residual = jnp.where(first, start, 0.0)

    def total(x):
        return jnp.sum(jnp.sum(x, 0, keepdims=True), 1, keepdims=True)

    def applied(v):
        return (
            diagonal * v
            + beside * pltpu.roll(v, 7, 0)
            + pltpu.roll(beside * v, 1, 0)
        )

    image = applied(residual)
    norm, product = total(residual * residual), total(residual * image)
    size = norm / product
    direction, along, y = residual, image, size * residual
    for i in range(5):
        residual = residual - size * along
        image = applied(residual)
        new, product = total(residual * residual), total(residual * image)
        growth = new / norm
        size = new / (product - growth * new / size)
        direction, along = residual + growth * direction, image + growth * along
        y, norm = y + size * direction, new
    mine = lane_index((8, LANES)) == place_ref[0]
    own = jnp.sum(jnp.where(mine, y * table[24:32], 0.0), 1, keepdims=True)
    lane = lane_index((8, LANES))
    last_row = row_index((8, LANES)) == 7

    def leaving(half):
        rows = pl.ds(64 * OUT_TILES * half, 64 * OUT_TILES)
        return pltpu.make_async_copy(packed_ref.at[rows], out_ref.at[rows], out_sems.at[half])

    for half in (1, 0):
        for slot in range(7):
            arriving(slot, half).wait()
        x = basis_ref[0, :, half]
        for i in range(6):
            x = x + own[i : i + 1, :][None] * basis_ref[1 + i, :, half]
        x_ref[:, half] = x

        def node_rows(c, r, k):
            block = x_ref[c, half, 8 * (r % 2) : 8 * (r % 2) + 8, tile_of(k)]
            if r < 2:
                return block
            beyond = x_ref[c, 1, 0:1, tile_of(k)] if half == 0 else 0.0
            return jnp.where(last_row, beyond, pltpu.roll(block, 7, 0))

        def put(t, tile, block):
            start = OUT_TILES * (64 * half + t) + tile
            packed_ref[pl.ds(start, 8, stride=8 * OUT_TILES), :] = block

        for u in range(4):
            even, odd = 2 * u, 2 * u + 1
            for c in range(3):
                for r in range(3):
                    put(even, 4 * c + r, node_rows(c, r, 3 * u))
                    put(odd, 4 * c + r, node_rows(c, r, 3 * u + 2))
                low, high = node_rows(c, 0, 3 * u + 1), node_rows(c, 1, 3 * u + 1)
                put(even, 4 * c + 3, jnp.where(lane < 64, low, pltpu.roll(high, 64, 1)))
                put(odd, 4 * c + 3, jnp.where(lane < 64, pltpu.roll(low, 64, 1), high))
            extra = [node_rows(c, 2, 3 * u + 1) for c in range(3)]
            put(even, OUT_TAIL, jnp.where(lane < 64, extra[0], pltpu.roll(extra[1], 64, 1)))
            put(odd, OUT_TAIL, jnp.where(lane < 64, pltpu.roll(extra[0], 64, 1), extra[1]))
            for parity, t in ((0, even), (1, odd)):
                block = extra[2] if parity == 0 else pltpu.roll(extra[2], 64, 1)
                following = (t + 1) % 8
                k, source = 3 * (following // 2) + following % 2, 64 * (following % 2)
                for c in range(3):
                    for r in range(3):
                        target = 64 + 3 * c + r
                        value = pltpu.roll(node_rows(c, r, k), (target - source) % LANES, 1)
                        block = jnp.where(lane == target, value, block)
                put(t, OUT_TAIL + 1, block)
        leaving(half).start()
    for half in range(2):
        leaving(half).wait()


def finish_kernel(parity_ref, stiff_ref, recv_ref, stress_ref, shear_far_ref, relax_far_ref,
                  x_out_ref, stress_out_ref, x_ref, new_ref, matrix_ref, shear_ref, relax_ref,
                  first_ref, x_sems, sems):
    shear_arriving = pltpu.make_async_copy(shear_far_ref, shear_ref, sems.at[4])
    relax_arriving = pltpu.make_async_copy(relax_far_ref, relax_ref, sems.at[5])
    shear_arriving.start()
    relax_arriving.start()
    parity = parity_ref[0]
    wide = pl.ds(pl.multiple_of(64 * parity, 64), 128)
    narrow = pl.ds(pl.multiple_of(128 * (1 - parity), 64), 64)

    def block(k):
        return jnp.transpose(recv_ref[pl.ds(k, LANES, stride=OUT_TILES), :])

    def x_leaving(c):
        return pltpu.make_async_copy(x_ref.at[c, 0:2, 0:COLS], x_out_ref.at[c], x_sems.at[c])

    def leaving(part):
        rows = pl.ds((0, 64, 128, 160)[part], (64, 64, 32, 32)[part])
        return pltpu.make_async_copy(
            new_ref.at[:, :, rows], stress_out_ref.at[:, :, rows], sems.at[part]
        )

    for c in range(3):
        for r in range(3):
            x_ref[c, r, wide, :] = block(4 * c + r)
        rest = block(4 * c + 3)
        x_ref[c, 0, narrow, :] = rest[0:64]
        x_ref[c, 1, narrow, :] = rest[64:128]
        x_leaving(c).start()
    rest = block(OUT_TAIL)
    x_ref[0, 2, narrow, :] = rest[0:64]
    x_ref[1, 2, narrow, :] = rest[64:128]
    rest = block(OUT_TAIL + 1)
    x_ref[2, 2, narrow, :] = rest[0:64]
    for c in range(3):
        for r in range(3):
            x_ref[c, r, COLS : COLS + 1, :] = rest[64 + 3 * c + r : 65 + 3 * c + r]

    lane = lane_index((16, 192))
    same = (lane % 16) == row_index((16, 192))
    for a in range(12):
        line = jnp.zeros((16, 192), f32)
        for b in range(12):
            line = jnp.where(lane // 16 == b, stiff_ref[12 * a + b], line)
        high, low = split(jnp.where(same, line, 0.0))
        for k, piece in enumerate((high, high, low)):
            matrix_ref[16 * a : 16 * a + 16, 256 * k : 256 * k + 192] = piece
            matrix_ref[16 * a : 16 * a + 16, 256 * k + 192 : 256 * k + 256] = jnp.zeros(
                (16, 64), bf16
            )

    pad = jnp.zeros((64, 2 * LANES), bf16)

    def forces(n):
        corners = []
        for c in range(3):
            for dr in range(2):
                for dh in range(2):
                    span = slice(16 * n + dh, 16 * n + dh + 16)
                    corners.append(
                        jnp.concatenate([x_ref[c, dr, span, :], x_ref[c, 1 + dr, span, :]], 1)
                    )
        high, low = split(jnp.concatenate(corners, 0))
        return mm(matrix_ref[...], jnp.concatenate([high, pad, low, pad, high, pad], 0))

    def store(n, force):
        rows = slice(16 * n, 16 * n + 16)
        for r in range(2):
            relax = relax_ref[r, rows, :]
            share = 1.0 / (1.0 + 0.5 * relax)
            eff, kept = shear_ref[r, rows, :] * share, (1.0 - 0.5 * relax) * share
            for a in range(12):
                new_ref[a, r, rows, :] = (
                    kept * stress_ref[a, r, rows, :]
                    + eff * force[16 * a : 16 * a + 16, tile_of(r)]
                )

    for n in range(4):
        first_ref[n] = forces(n)
    shear_arriving.wait()
    relax_arriving.wait()
    for n in range(4):
        store(n, first_ref[n])
    leaving(0).start()
    for n in range(4, COLS // 16):
        store(n, forces(n))
        if n in (7, 9, 11):
            leaving((n - 5) // 2).start()
    for c in range(3):
        x_leaving(c).wait()
    for part in range(4):
        leaving(part).wait()


def potential_kernel(recv_ref, out_ref):
    blocks = [jnp.transpose(recv_ref[pl.ds(k, LANES, stride=MID_TILES), :]) for k in range(3)]
    lines = jnp.concatenate(blocks, 0)
    for part in range(2):
        for r in range(2):
            start = 96 * (2 * part + r)
            out_ref[:, r, tile_of(part)] = lines[start : start + 96]


def whole(shape):
    return pl.BlockSpec(shape, lambda *_: (0,) * len(shape))


smem = pl.BlockSpec(memory_space=pltpu.SMEM)


def far_memory(x):
    return pltpu.with_memory_space_constraint(x, pltpu.HBM)


def exchanged(lines):
    count = lines.shape[0]
    rows = lines.reshape(LANES, 1, count)
    return lax.all_to_all(rows, ALL, 0, 0, tiled=True).reshape(count, LANES)


def params(mib):
    return pltpu.CompilerParams(vmem_limit_bytes=mib * 2**20)


def body(load, previous, stress_old, shear_modulus, relaxation, density_jump, element_stiffness,
         degree_slots):
    tile_place = lax.axis_index(TILE)
    place = (lax.axis_index(CAP) * 8 + tile_place).astype(jnp.int32).reshape(1)
    parity = (tile_place % 2).astype(jnp.int32).reshape(1)
    stiff = element_stiffness.reshape(144)
    slots = jnp.pad(degree_slots.reshape(8, 96), ((0, 0), (0, 32)), constant_values=-1)
    (fh, fl), (th, tl), twiddle = transform_tables()
    ratio, scale, radius = radial_tables()

    packed = pl.pallas_call(
        pack_kernel,
        in_specs=[smem, smem] + [pl.BlockSpec(memory_space=pl.ANY)] * 5,
        out_specs=pl.BlockSpec(memory_space=pltpu.VMEM),
        out_shape=pltpu.HBM((IN_TILES * LANES, LANES), f32),
        scratch_shapes=[
            pltpu.VMEM((3, 2, COLS, LANES), f32),
            pltpu.VMEM((3, 2, COLS, LANES), f32),
            pltpu.VMEM((12, 2, COLS, LANES), f32),
            pltpu.VMEM((2, COLS, LANES), f32),
            pltpu.VMEM((2, COLS, LANES), f32),
            pltpu.VMEM((3, COLS, LANES), f32),
            pltpu.VMEM((256, LANES), f32),
            pltpu.SemaphoreType.DMA((11,)),
        ],
        compiler_params=params(12),
    )(parity, *[far_memory(x) for x in (density_jump, load, previous, stress_old, shear_modulus, relaxation)])
    received = exchanged(packed)

    basis, sent = pl.pallas_call(
        functools.partial(section_kernel, radius=[float(x) for x in radius]),
        in_specs=[smem] + [pl.BlockSpec(memory_space=pltpu.VMEM)] * 9,
        out_specs=[pl.BlockSpec(memory_space=pl.ANY), pl.BlockSpec(memory_space=pltpu.VMEM)],
        out_shape=[
            pltpu.HBM((7, 96, HRING), f32),
            pltpu.HBM((MID_TILES * LANES, LANES), f32),
        ],
        scratch_shapes=[
            pltpu.VMEM((8, 96, HRING), f32),
            pltpu.SemaphoreType.DMA((7,)),
            pltpu.VMEM((2, 32, HRING), f32),
            pltpu.VMEM((2, 384, 256), bf16),
            pltpu.VMEM((192, LDEG), bf16),
            pltpu.VMEM((192, LDEG), bf16),
            pltpu.VMEM((2, 256, HRING), bf16),
            pltpu.VMEM((2, 8, HRING), f32),
            pltpu.VMEM((96, HRING), f32),
            pltpu.VMEM((512, LANES), f32),
            pltpu.VMEM((NR, 8, 256), f32),
        ],
        compiler_params=params(20),
    )(stiff, received, slots, fh, fl, th, tl, twiddle, ratio, scale)
    shared = exchanged(sent)

    back = pl.pallas_call(
        solve_kernel,
        grid=(1,),
        in_specs=[
            smem,
            whole((MID_TILES * LANES, LANES)),
            pl.BlockSpec(memory_space=pl.ANY),
        ],
        out_specs=pl.BlockSpec(memory_space=pl.ANY),
        out_shape=pltpu.HBM((OUT_TILES * LANES, LANES), f32),
        scratch_shapes=[
            pltpu.VMEM((3, 2, 16, HRING), f32),
            pltpu.VMEM((7, 3, 2, 16, HRING), f32),
            pltpu.VMEM((OUT_TILES * LANES, LANES), f32),
            pltpu.SemaphoreType.DMA((2, 7)),
            pltpu.SemaphoreType.DMA((2,)),
        ],
        compiler_params=params(12),
    )(place, shared, far_memory(basis.reshape(7, 3, 2, 16, HRING)))
    returned = exchanged(back)

    potential = pl.pallas_call(
        potential_kernel,
        grid=(1,),
        in_specs=[whole((MID_TILES * LANES, LANES))],
        out_specs=whole((96, 2, 256)),
        out_shape=jax.ShapeDtypeStruct((96, 2, 256), f32),
        compiler_params=params(4),
    )(shared)

    displacement, stress_new = pl.pallas_call(
        finish_kernel,
        in_specs=[smem, smem]
        + [pl.BlockSpec(memory_space=pltpu.VMEM)] * 2
        + [pl.BlockSpec(memory_space=pl.ANY)] * 2,
        out_specs=[pl.BlockSpec(memory_space=pl.ANY)] * 2,
        out_shape=[
            jax.ShapeDtypeStruct((3, 2, COLS, LANES), f32),
            jax.ShapeDtypeStruct((12, 2, COLS, LANES), f32),
        ],
        scratch_shapes=[
            pltpu.VMEM((3, 3, COLS + 8, LANES), f32),
            pltpu.VMEM((12, 2, COLS, LANES), f32),
            pltpu.VMEM((192, 768), bf16),
            pltpu.VMEM((2, COLS, LANES), f32),
            pltpu.VMEM((2, COLS, LANES), f32),
            pltpu.VMEM((4, COLS, 2 * LANES), f32),
            pltpu.SemaphoreType.DMA((3,)),
            pltpu.SemaphoreType.DMA((6,)),
        ],
        compiler_params=params(12),
    )(parity, stiff, returned, stress_old, far_memory(shear_modulus), far_memory(relaxation))
    return displacement, stress_new, potential


def solution(mesh):
    torus = Mesh(mesh.devices.reshape(4, 4, 4, 2), ("cap_0", "cap_1", "tile_0", "tile_1"))
    return jax.shard_map(
        body,
        mesh=torus,
        in_specs=(
            P(None, CAP, TILE, None),
            P(None, CAP, TILE, None),
            P(None, CAP, TILE, None),
            P(CAP, TILE, None),
            P(CAP, TILE, None),
            P(CAP),
            P(),
            P(),
        ),
        out_specs=(P(None, CAP, TILE, None), P(None, CAP, TILE, None), P(TILE, CAP, None)),
        check_vma=False,
    )
```
